256 devices in a mesh: dp: 8 (over x, core), seq: 32 (over z, y).
Axes of the slice: x: 4, y: 4, z: 8, core: 2. Of those that a mesh axis runs over, the one named last changes fastest.
Arguments:
- projected: bfloat16 [8, 4096, 6144], P('dp', 'seq'), may hold values from -8 to 8
- out_weight: bfloat16 [2048, 2048], P(('dp', 'seq')), may hold values from -0.125 to 0.125
- upstream: bfloat16 [8, 4096, 2048], P('dp', 'seq'), may hold values from -6 to 6
- peak_mask: int32 [8, 4096], P('dp', 'seq'), may hold values 0 or 1
- block_layout: int32 [32, 32, 8], P('seq'), may hold values from 0 to 31, as said below
Outputs:
- attended: bfloat16 [8, 4096, 2048], P('dp', 'seq')
- projected_grad: bfloat16 [8, 4096, 6144], P('dp', 'seq')
- weight_grad: float32 [2048, 2048], P(('dp', 'seq'))
The draws below stay inside these ranges and needn't reach their ends.
Inputs may be any that keep to these rules, and one draw needn't show every extreme that they name: `block_layout`: for each head and each block row of queries, 8 distinct key-block indices, one of which is the row's own block.
All inputs are finite; a program needn't handle non-finite values. No bound on the sum of `peak_mask` on one device may be relied on, other than what follows from the above.
Results may differ from the reference program's by a relative error of at most 0.019.
Values may be sent and summed in bfloat16 or wider, within the bound.
A program may use at most 128 MiB of HBM per device.

```python
import math
import jax
import jax.numpy as jnp
from jax import lax

D = 2048
HEADS = 32
INNER = 2048
RUNS = 8
SEQ_LEN = 4096
BLOCKS = 32
KBLK = 8


def draw_block_layout(key, part):
    scale_top = 1 << 20
    random_rank = jax.random.randint(key, (HEADS, BLOCKS, BLOCKS), 0, scale_top)
    block_ids = jnp.arange(BLOCKS, dtype=jnp.int32)
    ranked = random_rank * BLOCKS + block_ids[None, None, :]
    ranked = jnp.where((block_ids[:, None] == block_ids[None, :])[None, :, :], scale_top * BLOCKS + BLOCKS, ranked)
    top_values, chosen = lax.top_k(ranked, KBLK)
    return chosen.astype(jnp.int32)


def draw_projected(key, part):
    key_base = jax.random.fold_in(key, 0)
    shape = (RUNS, SEQ_LEN, 3 * INNER)
    column = jnp.arange(3 * INNER)
    spread = jnp.where(column < 2 * INNER, 1.4, 3.0).astype(jnp.float32)
    base = jnp.clip(jax.random.normal(key_base, shape, jnp.float32), -4.0, 4.0) * spread
    return jnp.clip(base, -8.0, 8.0).astype(jnp.bfloat16)


def with_ends(entries, key, least, top_value):
    longest = entries.shape.index(max(entries.shape))
    spots = []
    for shift in (0, 1):
        where = [jax.random.randint(jax.random.fold_in(key, axis), (), 0, length) for axis, length in enumerate(entries.shape)]
        where[longest] = (where[longest] + shift) % entries.shape[longest]
        spots.append(tuple(where))
    return entries.at[spots[0]].set(least).at[spots[1]].set(top_value)


def levels(stream_key, extent, pieces, smallest, top_value):
    level, own = 1.0, jax.random.fold_in(stream_key, 6)
    for dim, shards_of in pieces:
        heights = jnp.exp(jax.random.uniform(jax.random.fold_in(own, dim), (shards_of,), jnp.float32, smallest / len(pieces), top_value / len(pieces)))
        level = level * jnp.repeat(heights, extent[dim] // shards_of).reshape([-1 if axis == dim else 1 for axis in range(len(extent))])
    return level


def centred(own_key, shape, scale, limit, pieces=(), held_as=jnp.bfloat16):
    entries = scale * jax.random.normal(own_key, shape, jnp.float32)
    if pieces:
        entries = entries * levels(own_key, shape, pieces, -0.22, 0.18)
    return jnp.clip(entries, -limit, limit).astype(held_as)


def setup_inputs(seed: int = 0) -> dict:
    splits = jax.random.split(jax.random.key(seed), 6)
    projected = draw_projected(jax.random.fold_in(splits[5], 71), 0)
    out_weight = centred(splits[1], (INNER, D), INNER ** -0.5, 0.125, ((0, 256),))
    upstream = centred(splits[2], (RUNS, SEQ_LEN, D), 1.0, 6.0, ((0, 8), (1, 32)))
    peak_mask = with_ends((jax.random.randint(splits[3], (RUNS, SEQ_LEN), 0, 2) < 1).astype(jnp.int32), jax.random.fold_in(splits[3], 1), 0, 1)
    block_layout = draw_block_layout(jax.random.fold_in(splits[5], 71), 0)
    return {"projected": projected, "out_weight": out_weight, "upstream": upstream, "peak_mask": peak_mask, "block_layout": block_layout}


def group_size(block_count, block_len):
    return math.gcd(block_count, max(1, 512 // block_len))

def block_forward(queries, key_rows, values, layout):
    seq_len, head_width = queries.shape
    block_count, key_count = layout.shape
    block_len = seq_len // block_count
    row_group = group_size(block_count, block_len)
    group_count = block_count // row_group
    score_scale = 1.0 / math.sqrt(head_width)
    key_blocks = key_rows.reshape(block_count, block_len, head_width)
    value_blocks = values.reshape(block_count, block_len, head_width)
    query_groups = queries.reshape(group_count, row_group, block_len, head_width)
    layout_groups = layout.reshape(group_count, row_group, key_count)

    def forward_group(packed):
        query_group, layout_group = packed
        key_group = key_blocks[layout_group].reshape(row_group, key_count * block_len, head_width)
        value_group = value_blocks[layout_group].reshape(row_group, key_count * block_len, head_width)
        scores = jnp.einsum('gqd,gkd->gqk', query_group.astype(jnp.float32), key_group.astype(jnp.float32)) * score_scale
        row_top = lax.optimization_barrier(jnp.max(scores, axis=-1, keepdims=True))
        log_total = row_top + jnp.log(lax.optimization_barrier(jnp.sum(jnp.exp(scores - row_top), axis=-1, keepdims=True)))
        soft_probs = jnp.exp(scores - log_total).astype(jnp.bfloat16)
        context = jnp.einsum('gqk,gkd->gqd', soft_probs.astype(jnp.float32), value_group.astype(jnp.float32)).astype(jnp.bfloat16)
        return (context, log_total[..., 0])
    context, log_total = lax.map(forward_group, (query_groups, layout_groups))
    return (context.reshape(seq_len, head_width), log_total.reshape(seq_len))

def block_backward(queries, key_rows, values, layout, context, log_total, grad_rows):
    seq_len, head_width = queries.shape
    block_count, key_count = layout.shape
    block_len = seq_len // block_count
    row_group = group_size(block_count, block_len)
    group_count = block_count // row_group
    score_scale = 1.0 / math.sqrt(head_width)
    key_blocks = key_rows.reshape(block_count, block_len, head_width)
    value_blocks = values.reshape(block_count, block_len, head_width)
    query_groups = queries.reshape(group_count, row_group, block_len, head_width)
    layout_groups = layout.reshape(group_count, row_group, key_count)
    context_groups = context.reshape(group_count, row_group, block_len, head_width)
    total_groups = log_total.reshape(group_count, row_group, block_len)
    grad_groups = grad_rows.reshape(group_count, row_group, block_len, head_width)

    def backward_group(running, packed):
        key_acc, value_acc = running
        query_group, layout_group, context_group, total_group, grad_group = packed
        key_group = key_blocks[layout_group].reshape(row_group, key_count * block_len, head_width)
        value_group = value_blocks[layout_group].reshape(row_group, key_count * block_len, head_width)
        scores = jnp.einsum('gqd,gkd->gqk', query_group.astype(jnp.float32), key_group.astype(jnp.float32)) * score_scale
        exact_probs = jnp.exp(scores - total_group[..., None])
        soft_probs = exact_probs.astype(jnp.bfloat16)
        grad_probs = jnp.einsum('gqd,gkd->gqk', grad_group.astype(jnp.float32), value_group.astype(jnp.float32))
        row_delta = lax.optimization_barrier(jnp.sum(grad_group.astype(jnp.float32) * context_group.astype(jnp.float32), axis=-1, keepdims=True))
        grad_scores = (exact_probs * (grad_probs - row_delta)).astype(jnp.bfloat16)
        grad_query = (jnp.einsum('gqk,gkd->gqd', grad_scores.astype(jnp.float32), key_group.astype(jnp.float32)) * score_scale).astype(jnp.bfloat16)
        key_part = jnp.einsum('gqk,gqd->gkd', grad_scores.astype(jnp.float32), query_group.astype(jnp.float32)) * score_scale
        value_part = jnp.einsum('gqk,gqd->gkd', soft_probs.astype(jnp.float32), grad_group.astype(jnp.float32))
        flat_index = layout_group.reshape(-1)
        key_acc = key_acc.at[flat_index].add(key_part.reshape(row_group * key_count, block_len, head_width))
        value_acc = value_acc.at[flat_index].add(value_part.reshape(row_group * key_count, block_len, head_width))
        return ((key_acc, value_acc), grad_query)
    initial = jnp.zeros((block_count, block_len, head_width), jnp.float32)
    (key_acc, value_acc), grad_query = lax.scan(backward_group, (initial, initial), (query_groups, layout_groups, context_groups, total_groups, grad_groups))
    grad_key = key_acc.reshape(seq_len, head_width).astype(jnp.bfloat16)
    grad_value = value_acc.reshape(seq_len, head_width).astype(jnp.bfloat16)
    return (grad_query.reshape(seq_len, head_width), grad_key, grad_value)

def reference(projected, out_weight, upstream, peak_mask, block_layout):
    run_count, seq_len, triple_width = projected.shape
    inner_width = triple_width // 3
    head_count = block_layout.shape[0]
    head_width = inner_width // head_count

    def one_run(weight_sum, packed):
        run_rows, run_grad, run_mask = packed
        split_heads = run_rows.reshape(seq_len, 3, head_count, head_width).transpose(2, 1, 0, 3)

        def head_forward(packed_head):
            triple_rows, layout = packed_head
            return block_forward(triple_rows[0], triple_rows[1], triple_rows[2], layout)
        context_heads, total_heads = lax.map(head_forward, (split_heads, block_layout))
        context = context_heads.transpose(1, 0, 2).reshape(seq_len, inner_width)
        attended = jnp.dot(context, out_weight, preferred_element_type=jnp.float32).astype(jnp.bfloat16)
        masked_grad = run_grad * run_mask[:, None].astype(run_grad.dtype)
        grad_context = jnp.dot(masked_grad, out_weight.T, preferred_element_type=jnp.float32).astype(jnp.bfloat16)
        weight_sum = weight_sum + jnp.dot(context.T, masked_grad, preferred_element_type=jnp.float32)
        grad_heads = grad_context.reshape(seq_len, head_count, head_width).transpose(1, 0, 2)

        def head_backward(packed_head):
            triple_rows, layout, context_head, total_head, grad_head = packed_head
            grad_query, grad_key, grad_value = block_backward(triple_rows[0], triple_rows[1], triple_rows[2], layout, context_head, total_head, grad_head)
            return jnp.stack([grad_query, grad_key, grad_value])
        grad_split = lax.map(head_backward, (split_heads, block_layout, context_heads, total_heads, grad_heads))
        projected_grad = grad_split.transpose(2, 1, 0, 3).reshape(seq_len, triple_width)
        return (weight_sum, (attended, projected_grad))
    initial = jnp.zeros((inner_width, out_weight.shape[1]), jnp.float32)
    weight_grad, (attended, projected_grad) = lax.scan(one_run, initial, (projected, upstream, peak_mask))
    return (attended, projected_grad, weight_grad)
```

```python
import jax
import jax.numpy as jnp
from jax import lax
from jax.experimental import pallas as pl
from jax.experimental.pallas import tpu as pltpu
from jax.sharding import PartitionSpec as P

HS = 64
SCALE = 0.125


def attention_kernel(layout, qkv, grad, out, kvn, acc, probs, scores):
    blocks, _, head, length = qkv.shape
    picks = layout.shape[1]
    pair = 2 * head

    def prepare(b, carry):
        kvn[b] = qkv[b, 1:3].reshape(pair, length).T
        acc[b] = jnp.zeros((length, pair), jnp.float32)
        return carry

    lax.fori_loop(0, blocks, prepare, 0)
    low = lax.broadcasted_iota(jnp.int32, (length, pair), 1) < head

    def row_block(r, carry):
        q = qkv[r, 0] * jnp.bfloat16(SCALE)
        g = grad[r]
        none = jnp.zeros_like(q)
        turned = jnp.concatenate([q, g], 0).T
        into_scores = jnp.concatenate(
            [jnp.concatenate([q, none], 1), jnp.concatenate([none, g], 1)], 0
        )
        into_keys = jnp.concatenate(
            [jnp.where(low, turned, 0), jnp.where(low, 0, turned)], 0
        )
        at = [layout[r, j] for j in range(picks)]
        top = None
        for j in range(picks):
            both = jnp.dot(kvn[at[j]], into_scores, preferred_element_type=jnp.float32)
            scores[j] = both
            part = jnp.max(both[:, :length].reshape(length // 8, 8, length), axis=0)
            top = part if top is None else jnp.maximum(top, part)
        top = jnp.max(top, axis=0, keepdims=True)
        total = jnp.zeros((8, length), jnp.float32)
        delta = jnp.zeros((8, length), jnp.float32)
        for j in range(picks):
            e = jnp.exp(scores[j, :, :length] - top)
            scores[j, :, :length] = e
            total += jnp.sum(e.reshape(length // 8, 8, length), axis=0)
            delta += jnp.sum((e * scores[j, :, length:]).reshape(length // 8, 8, length), axis=0)
        inverse = 1.0 / jnp.sum(total, axis=0, keepdims=True)
        delta = jnp.sum(delta, axis=0, keepdims=True) * inverse
        for j in range(picks):
            p = scores[j, :, :length] * inverse
            d = p * (scores[j, :, length:] - delta)
            rows = pl.ds(j * length, length)
            probs[rows, :length] = d.astype(jnp.bfloat16)
            probs[rows, length:] = p.astype(jnp.bfloat16)
        kvt = jnp.concatenate([qkv[at[j], 1:3].reshape(pair, length) for j in range(picks)], 1)
        both = jnp.dot(kvt, probs[...], preferred_element_type=jnp.float32)
        out[r, 0] = both[head:, length:].astype(jnp.bfloat16)
        out[r, 1] = (both[:head, :length] * SCALE).astype(jnp.bfloat16)
        for j in range(picks):
            acc[at[j]] += jnp.dot(
                probs[pl.ds(j * length, length), :], into_keys, preferred_element_type=jnp.float32
            )
        return carry

    lax.fori_loop(0, blocks, row_block, 0)

    def finish(b, carry):
        out[b, 2:4] = acc[b].T.astype(jnp.bfloat16).reshape(2, head, length)
        return carry

    lax.fori_loop(0, blocks, finish, 0)


def attention(layout, qkv, grad):
    blocks, _, head, length = qkv.shape
    picks = layout.shape[1]
    keys = picks * length
    vmem = pl.BlockSpec(memory_space=pltpu.VMEM)
    return pl.pallas_call(
        attention_kernel,
        name="attention",
        out_shape=jax.ShapeDtypeStruct((blocks, 4, head, length), jnp.bfloat16),
        in_specs=[pl.BlockSpec(memory_space=pltpu.SMEM), vmem, vmem],
        out_specs=vmem,
        scratch_shapes=[
            pltpu.VMEM((blocks, length, 2 * head), jnp.bfloat16),
            pltpu.VMEM((blocks, length, 2 * head), jnp.float32),
            pltpu.VMEM((keys, 2 * length), jnp.bfloat16),
            pltpu.VMEM((picks, length, 2 * length), jnp.float32),
        ],
        cost_estimate=pl.CostEstimate(
            flops=12 * blocks * length * keys * head,
            bytes_accessed=16 * blocks * length * head,
            transcendentals=blocks * length * keys,
        ),
        compiler_params=pltpu.CompilerParams(vmem_limit_bytes=32 << 20),
    )(layout, qkv, grad)


def on_device(projected, out_weight, upstream, peak_mask, block_layout):
    tokens = projected.shape[1]
    inner = projected.shape[2] // 3
    heads = inner // HS
    model = out_weight.shape[1]
    dp = lax.axis_size("dp")
    seq = lax.axis_size("seq")

    turned = projected[0].T.reshape(3, heads, HS, tokens).transpose(1, 0, 2, 3)
    qkv = lax.all_to_all(turned, "seq", split_axis=0, concat_axis=0, tiled=True)
    full_weight = lax.all_gather(out_weight, ("dp", "seq"), axis=0, tiled=True)
    masked_grad = upstream[0] * peak_mask[0][:, None].astype(jnp.bfloat16)
    run_grads = lax.all_gather(masked_grad, "dp", axis=0, tiled=True)
    grad_context = lax.dot_general(
        full_weight, masked_grad, (((1,), (1,)), ((), ())), preferred_element_type=jnp.float32
    ).astype(jnp.bfloat16)
    grad_heads = lax.all_to_all(
        grad_context.reshape(heads, HS, tokens), "seq", split_axis=0, concat_axis=0, tiled=True
    )
    results = attention(block_layout[0], qkv, grad_heads)
    back = lax.all_to_all(results, "seq", split_axis=0, concat_axis=0, tiled=True)
    context = back[:, 0].reshape(inner, tokens)
    projected_grad = back[:, 1:].transpose(3, 1, 0, 2).reshape(1, tokens, 3 * inner)
    attended = lax.dot_general(
        context, full_weight, (((0,), (0,)), ((), ())), preferred_element_type=jnp.float32
    ).astype(jnp.bfloat16)
    run_context = lax.all_to_all(
        context.reshape(dp, inner // dp, tokens), "dp", split_axis=0, concat_axis=0, tiled=True
    )
    run_context = run_context.transpose(1, 0, 2).reshape(inner // dp, dp * tokens)
    partial = jnp.dot(run_context, run_grads, preferred_element_type=jnp.float32)
    pieces = lax.all_to_all(
        partial.astype(jnp.bfloat16).reshape(seq, inner // (dp * seq), model),
        "seq",
        split_axis=0,
        concat_axis=0,
        tiled=True,
    )
    weight_grad = jnp.sum(pieces.astype(jnp.float32), axis=0)
    return (attended.reshape(1, tokens, model), projected_grad, weight_grad)


def solution(mesh):
    in_specs = (
        P("dp", "seq", None),
        P(("dp", "seq"), None),
        P("dp", "seq", None),
        P("dp", "seq"),
        P("seq", None, None),
    )
    out_specs = (P("dp", "seq", None), P("dp", "seq", None), P(("dp", "seq"), None))
    return jax.shard_map(
        on_device, mesh=mesh, in_specs=in_specs, out_specs=out_specs, check_vma=False
    )
```

```python
import jax
import jax.numpy as jnp
from jax import lax
from jax.experimental import pallas as pl
from jax.experimental.pallas import tpu as pltpu
from jax.sharding import PartitionSpec as P

HS = 64
SCALE = 0.125


def attention_kernel(layout, qkv, grad, out, kvn, acc, probs, scores):
    blocks, _, head, length = qkv.shape
    picks = layout.shape[1]
    pair = 2 * head

    def prepare(b, carry):
        kvn[b] = qkv[b, 1:3].reshape(pair, length).T
        acc[b] = jnp.zeros((length, pair), jnp.float32)
        return carry

    lax.fori_loop(0, blocks, prepare, 0)
    low = lax.broadcasted_iota(jnp.int32, (length, pair), 1) < head

    def row_block(r, carry):
        q = qkv[r, 0] * jnp.bfloat16(SCALE)
        g = grad[r]
        none = jnp.zeros_like(q)
        turned = jnp.concatenate([q, g], 0).T
        into_scores = jnp.concatenate(
            [jnp.concatenate([q, none], 1), jnp.concatenate([none, g], 1)], 0
        )
        into_keys = jnp.concatenate(
            [jnp.where(low, turned, 0), jnp.where(low, 0, turned)], 0
        )
        at = [layout[r, j] for j in range(picks)]
        top = None
        for j in range(picks):
            both = jnp.dot(kvn[at[j]], into_scores, preferred_element_type=jnp.float32)
            scores[j] = both
            part = jnp.max(both[:, :length].reshape(length // 8, 8, length), axis=0)
            top = part if top is None else jnp.maximum(top, part)
        top = jnp.max(top, axis=0, keepdims=True)
        total = jnp.zeros((8, length), jnp.float32)
        delta = jnp.zeros((8, length), jnp.float32)
        for j in range(picks):
            e = jnp.exp(scores[j, :, :length] - top)
            scores[j, :, :length] = e
            total += jnp.sum(e.reshape(length // 8, 8, length), axis=0)
            delta += jnp.sum((e * scores[j, :, length:]).reshape(length // 8, 8, length), axis=0)
        inverse = 1.0 / jnp.sum(total, axis=0, keepdims=True)
        delta = jnp.sum(delta, axis=0, keepdims=True) * inverse
        for j in range(picks):
            p = scores[j, :, :length] * inverse
            d = p * (scores[j, :, length:] - delta)
            rows = pl.ds(j * length, length)
            probs[rows, :length] = d.astype(jnp.bfloat16)
            probs[rows, length:] = p.astype(jnp.bfloat16)
        kvt = jnp.concatenate([qkv[at[j], 1:3].reshape(pair, length) for j in range(picks)], 1)
        both = jnp.dot(kvt, probs[...], preferred_element_type=jnp.float32)
        out[r, 0] = both[head:, length:].astype(jnp.bfloat16)
        out[r, 1] = (both[:head, :length] * SCALE).astype(jnp.bfloat16)
        for j in range(picks):
            acc[at[j]] += jnp.dot(
                probs[pl.ds(j * length, length), :], into_keys, preferred_element_type=jnp.float32
            )
        return carry

    lax.fori_loop(0, blocks, row_block, 0)

    def finish(b, carry):
        out[b, 2:4] = acc[b].T.astype(jnp.bfloat16).reshape(2, head, length)
        return carry

    lax.fori_loop(0, blocks, finish, 0)


def attention(layout, qkv, grad):
    blocks, _, head, length = qkv.shape
    picks = layout.shape[1]
    keys = picks * length
    vmem = pl.BlockSpec(memory_space=pltpu.VMEM)
    return pl.pallas_call(
        attention_kernel,
        name="attention",
        out_shape=jax.ShapeDtypeStruct((blocks, 4, head, length), jnp.bfloat16),
        in_specs=[pl.BlockSpec(memory_space=pltpu.SMEM), vmem, vmem],
        out_specs=vmem,
        scratch_shapes=[
            pltpu.VMEM((blocks, length, 2 * head), jnp.bfloat16),
            pltpu.VMEM((blocks, length, 2 * head), jnp.float32),
            pltpu.VMEM((keys, 2 * length), jnp.bfloat16),
            pltpu.VMEM((picks, length, 2 * length), jnp.float32),
        ],
        cost_estimate=pl.CostEstimate(
            flops=12 * blocks * length * keys * head,
            bytes_accessed=16 * blocks * length * head,
            transcendentals=blocks * length * keys,
        ),
        compiler_params=pltpu.CompilerParams(vmem_limit_bytes=32 << 20),
    )(layout, qkv, grad)


def on_device(projected, out_weight, upstream, peak_mask, block_layout):
    tokens = projected.shape[1]
    inner = projected.shape[2] // 3
    heads = inner // HS
    model = out_weight.shape[1]
    dp = lax.axis_size("dp")
    seq = lax.axis_size("seq")

    turned = projected[0].T.reshape(3, heads, HS, tokens).transpose(1, 0, 2, 3)
    qkv = lax.all_to_all(turned, "seq", split_axis=0, concat_axis=0, tiled=True)
    run_weight = lax.all_gather(out_weight, "seq", axis=0, tiled=True)
    masked_grad = upstream[0] * peak_mask[0][:, None].astype(jnp.bfloat16)
    run_grads = lax.all_gather(masked_grad, "dp", axis=0, tiled=True)
    full_weight = lax.all_gather(run_weight, "dp", axis=0, tiled=True)
    grad_context = lax.dot_general(
        run_weight, run_grads, (((1,), (1,)), ((), ())), preferred_element_type=jnp.float32
    ).astype(jnp.bfloat16)
    grad_context = grad_context.reshape(inner // dp, dp, tokens).transpose(1, 0, 2)
    grad_context = lax.all_to_all(grad_context, "dp", split_axis=0, concat_axis=0, tiled=True)
    grad_heads = lax.all_to_all(
        grad_context.reshape(heads, HS, tokens), "seq", split_axis=0, concat_axis=0, tiled=True
    )
    results = attention(block_layout[0], qkv, grad_heads)
    back = lax.all_to_all(results, "seq", split_axis=0, concat_axis=0, tiled=True)
    context = back[:, 0].reshape(inner, tokens)
    projected_grad = back[:, 1:].transpose(3, 1, 0, 2).reshape(1, tokens, 3 * inner)
    attended = lax.dot_general(
        context, full_weight, (((0,), (0,)), ((), ())), preferred_element_type=jnp.float32
    ).astype(jnp.bfloat16)
    run_context = lax.all_to_all(
        context.reshape(dp, inner // dp, tokens), "dp", split_axis=0, concat_axis=0, tiled=True
    )
    run_context = run_context.transpose(1, 0, 2).reshape(inner // dp, dp * tokens)
    partial = jnp.dot(run_context, run_grads, preferred_element_type=jnp.float32)
    pieces = lax.all_to_all(
        partial.astype(jnp.bfloat16).reshape(seq, inner // (dp * seq), model),
        "seq",
        split_axis=0,
        concat_axis=0,
        tiled=True,
    )
    weight_grad = jnp.sum(pieces.astype(jnp.float32), axis=0)
    return (attended.reshape(1, tokens, model), projected_grad, weight_grad)


def solution(mesh):
    in_specs = (
        P("dp", "seq", None),
        P(("dp", "seq"), None),
        P("dp", "seq", None),
        P("dp", "seq"),
        P("seq", None, None),
    )
    out_specs = (P("dp", "seq", None), P("dp", "seq", None), P(("dp", "seq"), None))
    return jax.shard_map(
        on_device, mesh=mesh, in_specs=in_specs, out_specs=out_specs, check_vma=False
    )
```

```python
import jax
import jax.numpy as jnp
from jax import lax
from jax.experimental import pallas as pl
from jax.experimental.pallas import tpu as pltpu
from jax.sharding import PartitionSpec as P

HS = 64
SCALE = 0.125


def attention_kernel(layout, qkv, grad, out, kvn, acc, probs, scores):
    blocks, _, head, length = qkv.shape
    picks = layout.shape[1]
    pair = 2 * head

    def prepare(b, carry):
        kvn[b] = qkv[b, 1:3].reshape(pair, length).T
        acc[b] = jnp.zeros((length, pair), jnp.float32)
        return carry

    lax.fori_loop(0, blocks, prepare, 0)
    low = lax.broadcasted_iota(jnp.int32, (length, pair), 1) < head

    def row_block(r, carry):
        q = qkv[r, 0] * jnp.bfloat16(SCALE)
        g = grad[r]
        none = jnp.zeros_like(q)
        turned = jnp.concatenate([q, g], 0).T
        into_scores = jnp.concatenate(
            [jnp.concatenate([q, none], 1), jnp.concatenate([none, g], 1)], 0
        )
        into_keys = jnp.concatenate(
            [jnp.where(low, turned, 0), jnp.where(low, 0, turned)], 0
        )
        at = [layout[r, j] for j in range(picks)]
        top = None
        for j in range(picks):
            both = jnp.dot(kvn[at[j]], into_scores, preferred_element_type=jnp.float32)
            scores[j] = both
            part = jnp.max(both[:, :length].reshape(length // 8, 8, length), axis=0)
            top = part if top is None else jnp.maximum(top, part)
        top = jnp.max(top, axis=0, keepdims=True)
        total = jnp.zeros((8, length), jnp.float32)
        delta = jnp.zeros((8, length), jnp.float32)
        for j in range(picks):
            e = jnp.exp(scores[j, :, :length] - top)
            scores[j, :, :length] = e
            total += jnp.sum(e.reshape(length // 8, 8, length), axis=0)
            delta += jnp.sum((e * scores[j, :, length:]).reshape(length // 8, 8, length), axis=0)
        inverse = 1.0 / jnp.sum(total, axis=0, keepdims=True)
        delta = jnp.sum(delta, axis=0, keepdims=True) * inverse
        for j in range(picks):
            p = scores[j, :, :length] * inverse
            d = p * (scores[j, :, length:] - delta)
            rows = pl.ds(j * length, length)
            probs[rows, :length] = d.astype(jnp.bfloat16)
            probs[rows, length:] = p.astype(jnp.bfloat16)
        kvt = jnp.concatenate([qkv[at[j], 1:3].reshape(pair, length) for j in range(picks)], 1)
        both = jnp.dot(kvt, probs[...], preferred_element_type=jnp.float32)
        out[r, 0] = both[head:, length:].astype(jnp.bfloat16)
        out[r, 1] = (both[:head, :length] * SCALE).astype(jnp.bfloat16)
        for j in range(picks):
            acc[at[j]] += jnp.dot(
                probs[pl.ds(j * length, length), :], into_keys, preferred_element_type=jnp.float32
            )
        return carry

    lax.fori_loop(0, blocks, row_block, 0)

    def finish(b, carry):
        out[b, 2:4] = acc[b].T.astype(jnp.bfloat16).reshape(2, head, length)
        return carry

    lax.fori_loop(0, blocks, finish, 0)


def attention(layout, qkv, grad):
    blocks, _, head, length = qkv.shape
    picks = layout.shape[1]
    keys = picks * length
    vmem = pl.BlockSpec(memory_space=pltpu.VMEM)
    return pl.pallas_call(
        attention_kernel,
        name="attention",
        out_shape=jax.ShapeDtypeStruct((blocks, 4, head, length), jnp.bfloat16),
        in_specs=[pl.BlockSpec(memory_space=pltpu.SMEM), vmem, vmem],
        out_specs=vmem,
        scratch_shapes=[
            pltpu.VMEM((blocks, length, 2 * head), jnp.bfloat16),
            pltpu.VMEM((blocks, length, 2 * head), jnp.float32),
            pltpu.VMEM((keys, 2 * length), jnp.bfloat16),
            pltpu.VMEM((picks, length, 2 * length), jnp.float32),
        ],
        cost_estimate=pl.CostEstimate(
            flops=12 * blocks * length * keys * head,
            bytes_accessed=16 * blocks * length * head,
            transcendentals=blocks * length * keys,
        ),
        compiler_params=pltpu.CompilerParams(vmem_limit_bytes=32 << 20),
    )(layout, qkv, grad)


MESH = pl.DeviceIdType.MESH


def place():
    d, s = lax.axis_index("dp"), lax.axis_index("seq")
    return d, d // 2, d % 2, s, s // 4, s % 4


def shifted(z, y, k):
    return (z + k // 4) % 8 * 4 + (y + k % 4) % 4


def gather_kernel(
    weight, rows, upstream, mask, qkv, grad, grads, run_weight, turned, sent,
    w_send, w_recv, m_send, m_recv, q_send, q_recv, g_send, g_recv,
):
    d, x, core, s, z, y = place()
    tokens, model = upstream.shape
    heads, _, head, _ = qkv.shape
    seq, runs, depth = heads, grads.shape[0], weight.shape[0]
    own = d * (heads // runs)

    def to(dp, at):
        return {"device_id": (dp, at), "device_id_type": MESH}

    barrier = pltpu.get_barrier_semaphore()

    def greet_seq(k, carry):
        pl.semaphore_signal(barrier, inc=1, **to(d, shifted(z, y, k)))
        return carry

    def greet_dp(k, carry):
        pl.semaphore_signal(barrier, inc=1, **to((d + k) % runs, s))
        return carry

    def greet_grad(k, carry):
        @pl.when((s // 4 != d) | (k != s))
        def _():
            pl.semaphore_signal(barrier, inc=1, **to(s // 4, k))

        return carry

    lax.fori_loop(1, seq, greet_seq, 0)
    lax.fori_loop(1, runs, greet_dp, 0)
    lax.fori_loop(0, seq, greet_grad, 0)
    among = jnp.where(s // 4 == d, 1, 0)
    pl.semaphore_wait(barrier, seq - 1 + runs - 1 + seq - among)

    def weight_rows(at):
        return run_weight.at[pl.ds(pl.multiple_of(at * depth, depth), depth)]

    run_weight[pl.ds(pl.multiple_of(s * depth, depth), depth), :] = weight[...]

    def weight_copy(at, k, peer):
        return pltpu.make_async_remote_copy(
            weight_rows(at), weight_rows(at), w_send.at[k], w_recv.at[at], **to(d, peer)
        )

    def weight_z(k, carry):
        weight_copy(s, k, (z + k) % 8 * 4 + y).start()
        return carry

    lax.fori_loop(1, 8, weight_z, 0)

    column = jnp.broadcast_to(mask[...].astype(jnp.float32), (tokens, tokens)).T.astype(jnp.bfloat16)
    for i in range(model // tokens):
        part = slice(i * tokens, (i + 1) * tokens)
        grads[d, :, part] = upstream[:, part] * column

    def grad_copy(run, k, peer):
        return pltpu.make_async_remote_copy(
            grads.at[run], grads.at[run], m_send.at[k], m_recv.at[run], **to(peer, s)
        )

    def chip(k):
        return (x + k) % 4 * 2

    def grads_x(k, carry):
        grad_copy(d, k, chip(k) + core).start()
        return carry

    lax.fori_loop(1, 4, grads_x, 0)
    grad_copy(d, 0, d + 1 - 2 * core).start()

    def turn(pair, carry):
        for c in range(3):
            at = pl.multiple_of(c * (heads * head) + pair * 2 * head, 2 * head)
            both = rows[:, pl.ds(at, 2 * head)].T
            turned[2 * pair, c] = both[:head]
            turned[2 * pair + 1, c] = both[head:]
        return carry

    lax.fori_loop(0, heads // 2, turn, 0)

    def weight_y(k, carry):
        at = (z + k) % 8 * 4 + y

        @pl.when(k > 0)
        def _():
            weight_copy(at, 0, s).wait_recv()

        for i in range(1, 4):
            weight_copy(at, 8 * i + k, z * 4 + (y + i) % 4).start()
        return carry

    lax.fori_loop(0, 8, weight_y, 0)

    def qkv_copy(k):
        peer = shifted(z, y, k)
        return pltpu.make_async_remote_copy(
            turned.at[peer], qkv.at[s], q_send.at[k], q_recv.at[k], **to(d, peer)
        )

    def send_qkv(k, carry):
        qkv_copy(k).start()
        return carry

    lax.fori_loop(1, seq, send_qkv, 0)
    qkv[s] = turned[s]

    def weight_wait(k, carry):
        for i in range(1, 4):
            weight_copy(k * 4 + (y + i) % 4, 0, s).wait_recv()
        return carry

    lax.fori_loop(0, 8, weight_wait, 0)

    def context_copies(run):
        for j in range(heads // runs):
            yield own + j, pltpu.make_async_remote_copy(
                sent.at[run, j], grad.at[s], g_send.at[run, j], g_recv.at[s], **to(run, own + j)
            ), pltpu.make_async_copy(sent.at[run, j], grad.at[s], g_recv.at[s])

    def one_run(run):
        value = lax.dot_general(
            run_weight[...], grads[run], (((1,), (1,)), ((), ())), preferred_element_type=jnp.float32
        )
        sent[run] = value.astype(jnp.bfloat16).reshape(heads // runs, head, tokens)
        for peer, remote, local in context_copies(run):
            here = (run == d) & (peer == s)

            @pl.when(here)
            def _():
                local.start()

            @pl.when(jnp.logical_not(here))
            def _():
                remote.start()

    def runs_near(k, carry):
        run = chip(k) + core

        @pl.when(k > 0)
        def _():
            grad_copy(run, 0, d).wait_recv()
            grad_copy(run, 3 + k, d + 1 - 2 * core).start()

        one_run(run)
        return carry

    lax.fori_loop(0, 4, runs_near, 0)

    def runs_other(k, carry):
        run = chip(k) + 1 - core
        grad_copy(run, 0, d).wait_recv()
        one_run(run)
        return carry

    lax.fori_loop(0, 4, runs_other, 0)

    def finish_qkv(k, carry):
        qkv_copy(k).wait()
        return carry

    lax.fori_loop(1, seq, finish_qkv, 0)

    def finish_grad(k, carry):
        pltpu.make_async_copy(grad.at[k], grad.at[k], g_recv.at[k]).wait()
        return carry

    lax.fori_loop(0, seq, finish_grad, 0)

    def finish_sent(run, carry):
        for peer, remote, _ in context_copies(run):
            @pl.when((run != d) | (peer != s))
            def _():
                remote.wait_send()

        return carry

    lax.fori_loop(0, runs, finish_sent, 0)

    def finish_weight(k, carry):
        weight_copy(s, k, s).wait_send()
        return carry

    lax.fori_loop(1, 32, finish_weight, 0)

    def finish_grads(k, carry):
        grad_copy(d, k, d).wait_send()
        return carry

    lax.fori_loop(0, 7, finish_grads, 0)


def gather(weight, rows, upstream, mask, heads, runs):
    tokens, model = upstream.shape
    depth = weight.shape[0]
    vmem = pl.BlockSpec(memory_space=pltpu.VMEM)
    dma = pltpu.SemaphoreType.DMA
    return pl.pallas_call(
        gather_kernel,
        name="gather",
        out_shape=(
            jax.ShapeDtypeStruct((heads, 3, HS, tokens), jnp.bfloat16),
            jax.ShapeDtypeStruct((heads, HS, tokens), jnp.bfloat16),
            jax.ShapeDtypeStruct((runs, tokens, model), jnp.bfloat16),
            jax.ShapeDtypeStruct((heads * depth, model), jnp.bfloat16),
        ),
        in_specs=[vmem] * 4,
        out_specs=(vmem,) * 4,
        scratch_shapes=[
            pltpu.VMEM((heads, 3, HS, tokens), jnp.bfloat16),
            pltpu.VMEM((runs, heads // runs, HS, tokens), jnp.bfloat16),
            dma((heads,)),
            dma((heads,)),
            dma((8,)),
            dma((runs,)),
            dma((heads,)),
            dma((heads,)),
            dma((runs, heads // runs)),
            dma((heads,)),
        ],
        cost_estimate=pl.CostEstimate(
            flops=2 * heads * depth * model * runs * tokens, bytes_accessed=16 << 20, transcendentals=0
        ),
        compiler_params=pltpu.CompilerParams(
            collective_id=0, has_side_effects=True, vmem_limit_bytes=40 << 20
        ),
    )(weight, rows, upstream, mask)


def scatter_kernel(
    results, weight, grads, attended, rows, weight_grad,
    context, pieces, swapped, partial, across, along,
    c_send, c_recv, q_send, q_recv, s_send, s_recv, a_send, a_recv, l_send, l_recv,
):
    d, _, _, s, z, y = place()
    heads, _, head, tokens = results.shape
    inner, model = weight.shape
    runs = grads.shape[0]
    depth = weight_grad.shape[0]
    share = inner // runs

    def to(dp, at):
        return {"device_id": (dp, at), "device_id_type": MESH}

    barrier = pltpu.get_barrier_semaphore()

    def greet_seq(k, carry):
        pl.semaphore_signal(barrier, inc=1, **to(d, shifted(z, y, k)))
        return carry

    def greet_dp(k, carry):
        pl.semaphore_signal(barrier, inc=1, **to((d + k) % runs, s))
        return carry

    lax.fori_loop(1, heads, greet_seq, 0)
    lax.fori_loop(1, runs, greet_dp, 0)
    pl.semaphore_wait(barrier, heads - 1 + runs - 1)

    def context_copy(k):
        peer = shifted(z, y, k)
        return pltpu.make_async_remote_copy(
            results.at[peer, 0], context.at[s], c_send.at[k], c_recv.at[k], **to(d, peer)
        )

    def piece_copy(k):
        peer = shifted(z, y, k)
        return pltpu.make_async_remote_copy(
            results.at[peer, pl.ds(1, 3)], pieces.at[s], q_send.at[k], q_recv.at[k], **to(d, peer)
        )

    def send_context(k, carry):
        context_copy(k).start()
        return carry

    def send_pieces(k, carry):
        piece_copy(k).start()
        return carry

    lax.fori_loop(1, heads, send_context, 0)
    lax.fori_loop(1, heads, send_pieces, 0)
    context[s] = results[s, 0]
    pieces[s] = results[s, 1:4]

    def wait_context(k, carry):
        context_copy(k).wait_recv()
        return carry

    lax.fori_loop(1, heads, wait_context, 0)

    group = heads // runs

    def swap_copy(k):
        peer = (d + k) % runs
        return pltpu.make_async_remote_copy(
            context.at[pl.ds(peer * group, group)], swapped.at[d], s_send.at[k], s_recv.at[k], **to(peer, s)
        )

    def send_swap(k, carry):
        swap_copy(k).start()
        return carry

    lax.fori_loop(1, runs, send_swap, 0)
    swapped[d] = context[pl.ds(d * group, group)]

    wide = 512

    def attend(i, carry):
        at = pl.ds(pl.multiple_of(i * wide, wide), wide)
        attended[:, at] = lax.dot_general(
            context[...].reshape(inner, tokens),
            weight[:, at],
            (((0,), (0,)), ((), ())),
            preferred_element_type=jnp.float32,
        ).astype(jnp.bfloat16)
        return carry

    lax.fori_loop(0, model // wide, attend, 0)

    def wait_swap(k, carry):
        swap_copy(k).wait_recv()
        return carry

    lax.fori_loop(1, runs, wait_swap, 0)

    def multiply(i, carry):
        at = pl.ds(pl.multiple_of(i * wide, wide), wide)
        total = jnp.zeros((share, wide), jnp.float32)
        for r in range(runs):
            total += jnp.dot(
                swapped[r].reshape(share, tokens), grads[r, :, at], preferred_element_type=jnp.float32
            )
        total = total.astype(jnp.bfloat16)
        for k in range(heads):
            partial[k % 4, k // 4, :, at] = total[k * depth : (k + 1) * depth]
        return carry

    lax.fori_loop(0, model // wide, multiply, 0)

    def across_copy(k):
        peer = (y + k) % 4
        return pltpu.make_async_remote_copy(
            partial.at[peer], across.at[k], a_send.at[k], a_recv.at[k], **to(d, z * 4 + peer)
        )

    for k in range(1, 4):
        across_copy(k).start()
    for k in range(1, 4):
        across_copy(k).wait_recv()

    def add_across(k, carry):
        total = partial[y, k].astype(jnp.float32)
        for i in range(1, 4):
            total += across[i, k].astype(jnp.float32)
        across[0, k] = total.astype(jnp.bfloat16)
        return carry

    def along_copy(k):
        peer = (z + k) % 8
        return pltpu.make_async_remote_copy(
            across.at[0, peer], along.at[k], l_send.at[k], l_recv.at[k], **to(d, peer * 4 + y)
        )

    def send_along(k, carry):
        along_copy(k).start()
        return carry

    lax.fori_loop(0, 8, add_across, 0)
    lax.fori_loop(1, 8, send_along, 0)

    def wait_pieces(k, carry):
        piece_copy(k).wait_recv()
        return carry

    lax.fori_loop(1, heads, wait_pieces, 0)

    def turn(pair, carry):
        for c in range(3):
            at = pl.multiple_of(c * inner + pair * 2 * head, 2 * head)
            both = jnp.concatenate([pieces[2 * pair, c], pieces[2 * pair + 1, c]], 0)
            rows[:, pl.ds(at, 2 * head)] = both.T
        return carry

    lax.fori_loop(0, heads // 2, turn, 0)

    def wait_along(k, carry):
        along_copy(k).wait_recv()
        return carry

    lax.fori_loop(1, 8, wait_along, 0)
    total = across[0, z].astype(jnp.float32)
    for k in range(1, 8):
        total += along[k].astype(jnp.float32)
    weight_grad[...] = total

    def finish_seq(k, carry):
        context_copy(k).wait_send()
        piece_copy(k).wait_send()
        return carry

    def finish_swap(k, carry):
        swap_copy(k).wait_send()
        return carry

    def finish_along(k, carry):
        along_copy(k).wait_send()
        return carry

    lax.fori_loop(1, heads, finish_seq, 0)
    lax.fori_loop(1, runs, finish_swap, 0)
    for k in range(1, 4):
        across_copy(k).wait_send()
    lax.fori_loop(1, 8, finish_along, 0)


def scatter(results, weight, grads, depth):
    heads, _, head, tokens = results.shape
    inner, model = weight.shape
    runs = grads.shape[0]
    bf16, dma = jnp.bfloat16, pltpu.SemaphoreType.DMA
    vmem = pl.BlockSpec(memory_space=pltpu.VMEM)
    return pl.pallas_call(
        scatter_kernel,
        name="scatter",
        out_shape=(
            jax.ShapeDtypeStruct((tokens, model), bf16),
            jax.ShapeDtypeStruct((tokens, 3 * inner), bf16),
            jax.ShapeDtypeStruct((depth, model), jnp.float32),
        ),
        in_specs=[vmem] * 3,
        out_specs=(vmem,) * 3,
        scratch_shapes=[
            pltpu.VMEM((heads, head, tokens), bf16),
            pltpu.VMEM((heads, 3, head, tokens), bf16),
            pltpu.VMEM((runs, heads // runs, head, tokens), bf16),
            pltpu.VMEM((4, 8, depth, model), bf16),
            pltpu.VMEM((4, 8, depth, model), bf16),
            pltpu.VMEM((8, depth, model), bf16),
            dma((heads,)), dma((heads,)), dma((heads,)), dma((heads,)),
            dma((runs,)), dma((runs,)), dma((4,)), dma((4,)), dma((8,)), dma((8,)),
        ],
        cost_estimate=pl.CostEstimate(
            flops=4 * inner * model * tokens, bytes_accessed=20 << 20, transcendentals=0
        ),
        compiler_params=pltpu.CompilerParams(
            collective_id=1, has_side_effects=True, vmem_limit_bytes=56 << 20
        ),
    )(results, weight, grads)


def on_device(projected, out_weight, upstream, peak_mask, block_layout):
    inner = projected.shape[2] // 3
    heads = inner // HS
    dp = lax.axis_size("dp")

    qkv, grad_heads, run_grads, run_weight = gather(
        out_weight, projected[0], upstream[0], peak_mask, heads, dp
    )
    full_weight = lax.all_gather(run_weight, "dp", axis=0, tiled=True)
    results = attention(block_layout[0], qkv, grad_heads)
    attended, projected_grad, weight_grad = scatter(
        results, full_weight, run_grads, out_weight.shape[0]
    )
    return (attended[None], projected_grad[None], weight_grad)


def solution(mesh):
    in_specs = (
        P("dp", "seq", None),
        P(("dp", "seq"), None),
        P("dp", "seq", None),
        P("dp", "seq"),
        P("seq", None, None),
    )
    out_specs = (P("dp", "seq", None), P("dp", "seq", None), P(("dp", "seq"), None))
    return jax.shard_map(
        on_device, mesh=mesh, in_specs=in_specs, out_specs=out_specs, check_vma=False
    )
```

```python
import jax
import jax.numpy as jnp
from jax import lax
from jax.experimental import pallas as pl
from jax.experimental.pallas import tpu as pltpu
from jax.sharding import PartitionSpec as P

HS = 64
SCALE = 0.125


def attention_kernel(layout, qkv, grad, out, kvn, acc, probs, scores):
    blocks, _, head, length = qkv.shape
    picks = layout.shape[1]
    pair = 2 * head

    def prepare(b, carry):
        kvn[b] = qkv[b, 1:3].reshape(pair, length).T
        acc[b] = jnp.zeros((length, pair), jnp.float32)
        return carry

    lax.fori_loop(0, blocks, prepare, 0)
    low = lax.broadcasted_iota(jnp.int32, (length, pair), 1) < head

    def row_block(r, carry):
        q = qkv[r, 0] * jnp.bfloat16(SCALE)
        g = grad[r]
        none = jnp.zeros_like(q)
        turned = jnp.concatenate([q, g], 0).T
        into_scores = jnp.concatenate(
            [jnp.concatenate([q, none], 1), jnp.concatenate([none, g], 1)], 0
        )
        into_keys = jnp.concatenate(
            [jnp.where(low, turned, 0), jnp.where(low, 0, turned)], 0
        )
        at = [layout[r, j] for j in range(picks)]
        top = None
        for j in range(picks):
            both = jnp.dot(kvn[at[j]], into_scores, preferred_element_type=jnp.float32)
            scores[j] = both
            part = jnp.max(both[:, :length].reshape(length // 8, 8, length), axis=0)
            top = part if top is None else jnp.maximum(top, part)
        top = jnp.max(top, axis=0, keepdims=True)
        total = jnp.zeros((8, length), jnp.float32)
        delta = jnp.zeros((8, length), jnp.float32)
        for j in range(picks):
            e = jnp.exp(scores[j, :, :length] - top)
            scores[j, :, :length] = e
            total += jnp.sum(e.reshape(length // 8, 8, length), axis=0)
            delta += jnp.sum((e * scores[j, :, length:]).reshape(length // 8, 8, length), axis=0)
        inverse = 1.0 / jnp.sum(total, axis=0, keepdims=True)
        delta = jnp.sum(delta, axis=0, keepdims=True) * inverse
        for j in range(picks):
            p = scores[j, :, :length] * inverse
            d = p * (scores[j, :, length:] - delta)
            rows = pl.ds(j * length, length)
            probs[rows, :length] = d.astype(jnp.bfloat16)
            probs[rows, length:] = p.astype(jnp.bfloat16)
        kvt = jnp.concatenate([qkv[at[j], 1:3].reshape(pair, length) for j in range(picks)], 1)
        both = jnp.dot(kvt, probs[...], preferred_element_type=jnp.float32)
        out[r, 0] = both[head:, length:].astype(jnp.bfloat16)
        out[r, 1] = (both[:head, :length] * SCALE).astype(jnp.bfloat16)
        for j in range(picks):
            acc[at[j]] += jnp.dot(
                probs[pl.ds(j * length, length), :], into_keys, preferred_element_type=jnp.float32
            )
        return carry

    lax.fori_loop(0, blocks, row_block, 0)

    def finish(b, carry):
        out[b, 2:4] = acc[b].T.astype(jnp.bfloat16).reshape(2, head, length)
        return carry

    lax.fori_loop(0, blocks, finish, 0)


def attention(layout, qkv, grad):
    blocks, _, head, length = qkv.shape
    picks = layout.shape[1]
    keys = picks * length
    vmem = pl.BlockSpec(memory_space=pltpu.VMEM)
    return pl.pallas_call(
        attention_kernel,
        name="attention",
        out_shape=jax.ShapeDtypeStruct((blocks, 4, head, length), jnp.bfloat16),
        in_specs=[pl.BlockSpec(memory_space=pltpu.SMEM), vmem, vmem],
        out_specs=vmem,
        scratch_shapes=[
            pltpu.VMEM((blocks, length, 2 * head), jnp.bfloat16),
            pltpu.VMEM((blocks, length, 2 * head), jnp.float32),
            pltpu.VMEM((keys, 2 * length), jnp.bfloat16),
            pltpu.VMEM((picks, length, 2 * length), jnp.float32),
        ],
        cost_estimate=pl.CostEstimate(
            flops=12 * blocks * length * keys * head,
            bytes_accessed=16 * blocks * length * head,
            transcendentals=blocks * length * keys,
        ),
        compiler_params=pltpu.CompilerParams(vmem_limit_bytes=32 << 20),
    )(layout, qkv, grad)


MESH = pl.DeviceIdType.MESH


def place():
    d, s = lax.axis_index("dp"), lax.axis_index("seq")
    return d, d // 2, d % 2, s, s // 4, s % 4


def shifted(z, y, k):
    along, across = k // 4, k % 4
    along = 4 + (1 - along % 2 * 2) * ((along + 1) // 2)
    across = 2 + (1 - across % 2 * 2) * ((across + 1) // 2)
    return (z + along) % 8 * 4 + (y + across) % 4


def gather_kernel(
    weight, rows_in, upstream_in, mask_in, qkv, grad, grads, run_weight,
    rows, upstream, mask, turned, sent, mixed,
    in_sem, w_send, w_recv, m_send, m_recv, q_send, q_recv, x_send, x_recv, g_send, g_recv,
):
    d, x, core, s, z, y = place()
    tokens, model = upstream.shape
    heads, _, head, _ = qkv.shape
    seq, runs, depth = heads, grads.shape[0], weight.shape[0]

    def to(dp, at):
        return {"device_id": (dp, at), "device_id_type": MESH}

    def weight_rows(at):
        return run_weight.at[pl.ds(pl.multiple_of(at * depth, depth), depth)]

    loads = [
        pltpu.make_async_copy(upstream_in, upstream, in_sem.at[0]),
        pltpu.make_async_copy(mask_in, mask, in_sem.at[1]),
        pltpu.make_async_copy(rows_in, rows, in_sem.at[2]),
        pltpu.make_async_copy(weight, weight_rows(s), in_sem.at[3]),
    ]
    for load in loads:
        load.start()
    barrier = pltpu.get_barrier_semaphore()

    def greet_seq(k, carry):
        pl.semaphore_signal(barrier, inc=1, **to(d, shifted(z, y, k)))
        return carry

    def greet_dp(k, carry):
        pl.semaphore_signal(barrier, inc=1, **to((d + k) % runs, s))
        return carry

    lax.fori_loop(0, seq - 1, greet_seq, 0)
    lax.fori_loop(1, runs, greet_dp, 0)
    loads[0].wait()
    loads[1].wait()
    column = jnp.broadcast_to(mask[...].astype(jnp.float32), (tokens, tokens)).T.astype(jnp.bfloat16)
    for i in range(model // tokens):
        part = slice(i * tokens, (i + 1) * tokens)
        grads[d, :, part] = upstream[:, part] * column

    def turn(pair, carry):
        for c in range(3):
            at = pl.multiple_of(c * (heads * head) + pair * 2 * head, 2 * head)
            both = rows[:, pl.ds(at, 2 * head)].T
            turned[2 * pair, c] = both[:head]
            turned[2 * pair + 1, c] = both[head:]
        return carry

    loads[2].wait()
    lax.fori_loop(0, heads // 2, turn, 0)
    loads[3].wait()

    pl.semaphore_wait(barrier, seq - 1 + runs - 1)

    def weight_copy(at, k, peer):
        return pltpu.make_async_remote_copy(
            weight_rows(at), weight_rows(at), w_send.at[k], w_recv.at[at], **to(d, peer)
        )

    def weight_z(k, carry):
        weight_copy(s, k, (z + k) % 8 * 4 + y).start()
        return carry

    lax.fori_loop(1, 8, weight_z, 0)

    def grad_copy(run, k, peer):
        return pltpu.make_async_remote_copy(
            grads.at[run], grads.at[run], m_send.at[k], m_recv.at[run], **to(peer, s)
        )

    def chip(k):
        return (x + k) % 4 * 2

    def grads_x(k, carry):
        grad_copy(d, k, chip(k) + core).start()
        return carry

    lax.fori_loop(1, 4, grads_x, 0)
    grad_copy(d, 0, d + 1 - 2 * core).start()

    def qkv_copy(k):
        peer = shifted(z, y, k)
        return pltpu.make_async_remote_copy(
            turned.at[peer], qkv.at[s], q_send.at[k], q_recv.at[k], **to(d, peer)
        )

    def send_qkv(k, carry):
        qkv_copy(k).start()
        return carry

    lax.fori_loop(0, seq - 1, send_qkv, 0)
    qkv[s] = turned[s]

    def weight_y(k, carry):
        at = (z + k) % 8 * 4 + y

        @pl.when(k > 0)
        def _():
            weight_copy(at, 0, s).wait_recv()

        for i in range(1, 4):
            weight_copy(at, 8 * i + k, z * 4 + (y + i) % 4).start()
        return carry

    lax.fori_loop(0, 8, weight_y, 0)

    def weight_wait(k, carry):
        for i in range(1, 4):
            weight_copy(k * 4 + (y + i) % 4, 0, s).wait_recv()
        return carry

    lax.fori_loop(0, 8, weight_wait, 0)

    def sent_copy(run, source):
        return pltpu.make_async_remote_copy(
            sent.at[run], mixed.at[source], x_send.at[run], x_recv.at[source], **to(run, s)
        )

    def one_run(run):
        value = lax.dot_general(
            run_weight[...], grads[run], (((1,), (1,)), ((), ())), preferred_element_type=jnp.float32
        )
        sent[run] = value.astype(jnp.bfloat16).reshape(heads // runs, head, tokens)

        @pl.when(run != d)
        def _():
            sent_copy(run, d).start()

    def runs_near(k, carry):
        run = chip(k) + core

        @pl.when(k > 0)
        def _():
            grad_copy(run, 0, d).wait_recv()
            grad_copy(run, 3 + k, d + 1 - 2 * core).start()

        one_run(run)
        return carry

    lax.fori_loop(0, 4, runs_near, 0)

    def runs_other(k, carry):
        run = chip(k) + 1 - core
        grad_copy(run, 0, d).wait_recv()
        one_run(run)
        return carry

    lax.fori_loop(0, 4, runs_other, 0)

    mixed[d] = sent[d]

    def wait_mixed(k, carry):
        sent_copy(d, (d + k) % runs).wait_recv()
        return carry

    lax.fori_loop(1, runs, wait_mixed, 0)

    def head_copy(k):
        peer = shifted(z, y, k)
        share = heads // runs
        return pltpu.make_async_remote_copy(
            mixed.at[peer // share, peer % share], grad.at[s], g_send.at[k], g_recv.at[k], **to(d, peer)
        )

    def send_head(k, carry):
        head_copy(k).start()
        return carry

    lax.fori_loop(0, seq - 1, send_head, 0)
    grad[s] = mixed[s // (heads // runs), s % (heads // runs)]

    def finish_seq(k, carry):
        qkv_copy(k).wait()
        head_copy(k).wait()
        return carry

    lax.fori_loop(0, seq - 1, finish_seq, 0)

    def finish_sent(k, carry):
        sent_copy((d + k) % runs, d).wait_send()
        return carry

    lax.fori_loop(1, runs, finish_sent, 0)

    def finish_weight(k, carry):
        weight_copy(s, k, s).wait_send()
        return carry

    lax.fori_loop(1, 32, finish_weight, 0)

    def finish_grads(k, carry):
        grad_copy(d, k, d).wait_send()
        return carry

    lax.fori_loop(0, 7, finish_grads, 0)


def gather(weight, rows, upstream, mask, heads, runs):
    tokens, model = upstream.shape
    depth = weight.shape[0]
    vmem = pl.BlockSpec(memory_space=pltpu.VMEM)
    dma = pltpu.SemaphoreType.DMA
    return pl.pallas_call(
        gather_kernel,
        name="gather",
        out_shape=(
            jax.ShapeDtypeStruct((heads, 3, HS, tokens), jnp.bfloat16),
            jax.ShapeDtypeStruct((heads, HS, tokens), jnp.bfloat16),
            jax.ShapeDtypeStruct((runs, tokens, model), jnp.bfloat16),
            jax.ShapeDtypeStruct((heads * depth, model), jnp.bfloat16),
        ),
        in_specs=[pl.BlockSpec(memory_space=pltpu.HBM)] * 4,
        out_specs=(vmem,) * 4,
        scratch_shapes=[
            pltpu.VMEM(rows.shape, jnp.bfloat16),
            pltpu.VMEM(upstream.shape, jnp.bfloat16),
            pltpu.VMEM(mask.shape, jnp.int32),
            pltpu.VMEM((heads, 3, HS, tokens), jnp.bfloat16),
            pltpu.VMEM((runs, heads // runs, HS, tokens), jnp.bfloat16),
            pltpu.VMEM((runs, heads // runs, HS, tokens), jnp.bfloat16),
            dma((4,)),
            dma((heads,)),
            dma((heads,)),
            dma((8,)),
            dma((runs,)),
            dma((heads,)),
            dma((heads,)),
            dma((runs,)),
            dma((runs,)),
            dma((heads,)),
            dma((heads,)),
        ],
        cost_estimate=pl.CostEstimate(
            flops=2 * heads * depth * model * runs * tokens, bytes_accessed=16 << 20, transcendentals=0
        ),
        compiler_params=pltpu.CompilerParams(
            collective_id=0, has_side_effects=True, vmem_limit_bytes=24 << 20
        ),
    )(weight, rows, upstream, mask)


def scatter_kernel(
    results, grads, context, pieces, weight_grad,
    swapped, partial, across, along,
    c_send, c_recv, q_send, q_recv, s_send, s_recv, a_send, a_recv, l_send, l_recv,
):
    d, _, _, s, z, y = place()
    heads, _, head, tokens = results.shape
    runs, _, model = grads.shape
    group = heads // runs
    share = group * head
    depth = weight_grad.shape[0]

    def to(dp, at):
        return {"device_id": (dp, at), "device_id_type": MESH}

    barrier = pltpu.get_barrier_semaphore()

    def greet_seq(k, carry):
        pl.semaphore_signal(barrier, inc=1, **to(d, shifted(z, y, k)))
        return carry

    def greet_dp(k, carry):
        pl.semaphore_signal(barrier, inc=1, **to((d + k) % runs, s))
        return carry

    lax.fori_loop(0, heads - 1, greet_seq, 0)
    lax.fori_loop(1, runs, greet_dp, 0)
    pl.semaphore_wait(barrier, heads - 1 + runs - 1)

    def context_copy(k):
        peer = shifted(z, y, k)
        return pltpu.make_async_remote_copy(
            results.at[peer, 0], context.at[s], c_send.at[k], c_recv.at[k], **to(d, peer)
        )

    def piece_copy(k):
        peer = shifted(z, y, k)
        return pltpu.make_async_remote_copy(
            results.at[peer, pl.ds(1, 3)], pieces.at[:, s], q_send.at[k], q_recv.at[k], **to(d, peer)
        )

    def send_context(k, carry):
        context_copy(k).start()
        return carry

    def send_pieces(k, carry):
        piece_copy(k).start()
        return carry

    lax.fori_loop(0, heads - 1, send_context, 0)
    context[s] = results[s, 0]
    pieces[:, s] = results[s, 1:4]

    def wait_context(k, carry):
        context_copy(k).wait_recv()
        return carry

    lax.fori_loop(0, heads - 1, wait_context, 0)
    lax.fori_loop(0, heads - 1, send_pieces, 0)

    def swap_copy(k):
        peer = (d + k) % runs
        return pltpu.make_async_remote_copy(
            context.at[pl.ds(peer * group, group)], swapped.at[d], s_send.at[k], s_recv.at[k], **to(peer, s)
        )

    def send_swap(k, carry):
        swap_copy(k).start()
        return carry

    lax.fori_loop(1, runs, send_swap, 0)
    swapped[d] = context[pl.ds(d * group, group)]

    def wait_swap(k, carry):
        swap_copy(k).wait_recv()
        return carry

    lax.fori_loop(1, runs, wait_swap, 0)

    wide = 512

    def multiply(i, carry):
        at = pl.ds(pl.multiple_of(i * wide, wide), wide)
        left = jnp.concatenate([swapped[r].reshape(share, tokens) for r in range(runs)], 1)
        right = grads[:, :, at].reshape(runs * tokens, wide)
        total = jnp.dot(left, right, preferred_element_type=jnp.float32).astype(jnp.bfloat16)
        for k in range(heads):
            partial[k % 4, k // 4, :, at] = total[k * depth : (k + 1) * depth]
        return carry

    lax.fori_loop(0, model // wide, multiply, 0)

    def across_copy(k):
        peer = (y + k) % 4
        return pltpu.make_async_remote_copy(
            partial.at[peer], across.at[k], a_send.at[k], a_recv.at[k], **to(d, z * 4 + peer)
        )

    for k in range(1, 4):
        across_copy(k).start()

    for k in range(1, 4):
        across_copy(k).wait_recv()

    def add_across(k, carry):
        total = partial[y, k].astype(jnp.float32)
        for i in range(1, 4):
            total += across[i, k].astype(jnp.float32)
        across[0, k] = total.astype(jnp.bfloat16)
        return carry

    def along_copy(k):
        peer = (z + k) % 8
        return pltpu.make_async_remote_copy(
            across.at[0, peer], along.at[k], l_send.at[k], l_recv.at[k], **to(d, peer * 4 + y)
        )

    def send_along(k, carry):
        along_copy(k).start()
        return carry

    lax.fori_loop(0, 8, add_across, 0)
    lax.fori_loop(1, 8, send_along, 0)

    def wait_pieces(k, carry):
        piece_copy(k).wait_recv()
        return carry

    def wait_along(k, carry):
        along_copy(k).wait_recv()
        return carry

    lax.fori_loop(1, 8, wait_along, 0)
    total = across[0, z].astype(jnp.float32)
    for k in range(1, 8):
        total += along[k].astype(jnp.float32)
    weight_grad[...] = total
    lax.fori_loop(0, heads - 1, wait_pieces, 0)

    def finish_seq(k, carry):
        context_copy(k).wait_send()
        piece_copy(k).wait_send()
        return carry

    def finish_swap(k, carry):
        swap_copy(k).wait_send()
        return carry

    def finish_along(k, carry):
        along_copy(k).wait_send()
        return carry

    lax.fori_loop(0, heads - 1, finish_seq, 0)
    lax.fori_loop(1, runs, finish_swap, 0)
    for k in range(1, 4):
        across_copy(k).wait_send()
    lax.fori_loop(1, 8, finish_along, 0)


def scatter(results, grads, depth):
    heads, _, head, tokens = results.shape
    runs, _, model = grads.shape
    bf16, dma = jnp.bfloat16, pltpu.SemaphoreType.DMA
    vmem = pl.BlockSpec(memory_space=pltpu.VMEM)
    return pl.pallas_call(
        scatter_kernel,
        name="scatter",
        out_shape=(
            jax.ShapeDtypeStruct((heads, head, tokens), bf16),
            jax.ShapeDtypeStruct((3, heads, head, tokens), bf16),
            jax.ShapeDtypeStruct((depth, model), jnp.float32),
        ),
        in_specs=[vmem] * 2,
        out_specs=(vmem,) * 3,
        scratch_shapes=[
            pltpu.VMEM((runs, heads // runs, head, tokens), bf16),
            pltpu.VMEM((4, 8, depth, model), bf16),
            pltpu.VMEM((4, 8, depth, model), bf16),
            pltpu.VMEM((8, depth, model), bf16),
            dma((heads,)), dma((heads,)), dma((heads,)), dma((heads,)),
            dma((runs,)), dma((runs,)), dma((4,)), dma((4,)), dma((8,)), dma((8,)),
        ],
        cost_estimate=pl.CostEstimate(
            flops=2 * heads * head * model * tokens, bytes_accessed=20 << 20, transcendentals=0
        ),
        compiler_params=pltpu.CompilerParams(
            collective_id=1, has_side_effects=True, vmem_limit_bytes=24 << 20
        ),
    )(results, grads)


def on_device(projected, out_weight, upstream, peak_mask, block_layout):
    inner = projected.shape[2] // 3
    heads = inner // HS
    dp = lax.axis_size("dp")

    qkv, grad_heads, run_grads, run_weight = gather(
        out_weight, projected[0], upstream[0], peak_mask, heads, dp
    )
    full_weight = lax.all_gather(run_weight, "dp", axis=0, tiled=True)
    results = attention(block_layout[0], qkv, grad_heads)
    context, projected_grad, weight_grad = scatter(results, run_grads, out_weight.shape[0])
    attended = lax.dot_general(
        context.reshape(inner, -1),
        full_weight,
        (((0,), (0,)), ((), ())),
        preferred_element_type=jnp.float32,
    ).astype(jnp.bfloat16)
    projected_grad = projected_grad.reshape(3 * inner, -1).T
    return (attended[None], projected_grad[None], weight_grad)


def solution(mesh):
    in_specs = (
        P("dp", "seq", None),
        P(("dp", "seq"), None),
        P("dp", "seq", None),
        P("dp", "seq"),
        P("seq", None, None),
    )
    out_specs = (P("dp", "seq", None), P("dp", "seq", None), P(("dp", "seq"), None))
    return jax.shard_map(
        on_device, mesh=mesh, in_specs=in_specs, out_specs=out_specs, check_vma=False
    )
```

```python
import jax
import jax.numpy as jnp
from jax import lax
from jax.experimental import pallas as pl
from jax.experimental.pallas import tpu as pltpu
from jax.sharding import PartitionSpec as P

HS = 64
SCALE = 0.125


def attention_kernel(layout, qkv, grad, out, kvn, acc, probs, scores):
    blocks, _, head, length = qkv.shape
    picks = layout.shape[1]
    pair = 2 * head
    eighths = length // 8

    def prepare(b, carry):
        kvn[b] = qkv[b, 1:3].reshape(pair, length).T
        acc[b] = jnp.zeros((length, pair), jnp.float32)
        return carry

    lax.fori_loop(0, blocks, prepare, 0, unroll=4)
    low = lax.broadcasted_iota(jnp.int32, (length, pair), 1) < head

    def picked(r):
        return [layout[r, j] for j in range(picks)]

    def scores_of(r, slot):
        q = qkv[r, 0] * jnp.bfloat16(SCALE)
        g = grad[r]
        none = jnp.zeros_like(q)
        into = jnp.concatenate([jnp.concatenate([q, none], 1), jnp.concatenate([none, g], 1)], 0)
        top = None
        for j, b in enumerate(picked(r)):
            both = jnp.dot(kvn[b], into, preferred_element_type=jnp.float32)
            scores[slot, j] = both
            part = jnp.max(both[:, :length].reshape(eighths, 8, length), axis=0)
            top = part if top is None else jnp.maximum(top, part)
        return jnp.max(top, axis=0, keepdims=True)

    def probs_of(slot, top):
        total = jnp.zeros((8, length), jnp.float32)
        delta = jnp.zeros((8, length), jnp.float32)
        for j in range(picks):
            e = jnp.exp(scores[slot, j, :, :length] - top)
            scores[slot, j, :, :length] = e
            total += jnp.sum(e.reshape(eighths, 8, length), axis=0)
            delta += jnp.sum((e * scores[slot, j, :, length:]).reshape(eighths, 8, length), axis=0)
        inverse = 1.0 / jnp.sum(total, axis=0, keepdims=True)
        delta = jnp.sum(delta, axis=0, keepdims=True) * inverse
        for j in range(picks):
            p = scores[slot, j, :, :length] * inverse
            d = p * (scores[slot, j, :, length:] - delta)
            rows = pl.ds(j * length, length)
            probs[slot, rows, :length] = d.astype(jnp.bfloat16)
            probs[slot, rows, length:] = p.astype(jnp.bfloat16)

    def results_of(r, slot):
        at = picked(r)
        kvt = jnp.concatenate([qkv[b, 1:3].reshape(pair, length) for b in at], 1)
        both = jnp.dot(kvt, probs[slot], preferred_element_type=jnp.float32)
        out[r, 0] = both[head:, length:].astype(jnp.bfloat16)
        out[r, 1] = (both[:head, :length] * SCALE).astype(jnp.bfloat16)
        turned = jnp.concatenate([qkv[r, 0] * jnp.bfloat16(SCALE), grad[r]], 0).T
        into = jnp.concatenate([jnp.where(low, turned, 0), jnp.where(low, 0, turned)], 0)
        for j, b in enumerate(at):
            acc[b] += jnp.dot(
                probs[slot, pl.ds(j * length, length), :], into, preferred_element_type=jnp.float32
            )

    probs_of(0, scores_of(0, 0))

    def two_rows(i, top):
        r = 2 * i
        later = scores_of(r + 2, 0)
        results_of(r, 0)
        probs_of(1, top)
        last = scores_of(r + 3, 1)
        results_of(r + 1, 1)
        probs_of(0, later)
        return last

    top = lax.fori_loop(0, blocks // 2 - 1, two_rows, scores_of(1, 1))
    results_of(blocks - 2, 0)
    probs_of(1, top)
    results_of(blocks - 1, 1)

    def finish(b, carry):
        out[b, 2:4] = acc[b].T.astype(jnp.bfloat16).reshape(2, head, length)
        return carry

    lax.fori_loop(0, blocks, finish, 0, unroll=4)


def attention(layout, qkv, grad):
    blocks, _, head, length = qkv.shape
    picks = layout.shape[1]
    keys = picks * length
    vmem = pl.BlockSpec(memory_space=pltpu.VMEM)
    return pl.pallas_call(
        attention_kernel,
        name="attention",
        out_shape=jax.ShapeDtypeStruct((blocks, 4, head, length), jnp.bfloat16),
        in_specs=[pl.BlockSpec(memory_space=pltpu.SMEM), vmem, vmem],
        out_specs=vmem,
        scratch_shapes=[
            pltpu.VMEM((blocks, length, 2 * head), jnp.bfloat16),
            pltpu.VMEM((blocks, length, 2 * head), jnp.float32),
            pltpu.VMEM((2, keys, 2 * length), jnp.bfloat16),
            pltpu.VMEM((2, picks, length, 2 * length), jnp.float32),
        ],
        cost_estimate=pl.CostEstimate(
            flops=12 * blocks * length * keys * head,
            bytes_accessed=16 * blocks * length * head,
            transcendentals=blocks * length * keys,
        ),
        compiler_params=pltpu.CompilerParams(vmem_limit_bytes=32 << 20),
    )(layout, qkv, grad)


MESH = pl.DeviceIdType.MESH


def place():
    d, s = lax.axis_index("dp"), lax.axis_index("seq")
    return d, d // 2, d % 2, s, s // 4, s % 4


def shifted(z, y, k):
    along, across = k // 4, k % 4
    along = 4 + (1 - along % 2 * 2) * ((along + 1) // 2)
    across = 2 + (1 - across % 2 * 2) * ((across + 1) // 2)
    return (z + along) % 8 * 4 + (y + across) % 4


def gather_kernel(
    weight, rows_in, upstream_in, mask_in, qkv, grad, grads, run_weight,
    rows, upstream, mask, turned, sent, mixed,
    in_sem, w_send, w_recv, m_send, m_recv, q_send, q_recv, x_send, x_recv, g_send, g_recv,
):
    d, x, core, s, z, y = place()
    tokens, model = upstream.shape
    heads, _, head, _ = qkv.shape
    seq, runs, depth = heads, grads.shape[0], weight.shape[0]

    def to(dp, at):
        return {"device_id": (dp, at), "device_id_type": MESH}

    def weight_rows(at):
        return run_weight.at[pl.ds(pl.multiple_of(at * depth, depth), depth)]

    loads = [
        pltpu.make_async_copy(upstream_in, upstream, in_sem.at[0]),
        pltpu.make_async_copy(mask_in, mask, in_sem.at[1]),
        pltpu.make_async_copy(rows_in, rows, in_sem.at[2]),
        pltpu.make_async_copy(weight, weight_rows(s), in_sem.at[3]),
    ]
    for load in loads:
        load.start()
    barrier = pltpu.get_barrier_semaphore()

    def greet_seq(k, carry):
        pl.semaphore_signal(barrier, inc=1, **to(d, shifted(z, y, k)))
        return carry

    def greet_dp(k, carry):
        pl.semaphore_signal(barrier, inc=1, **to((d + k) % runs, s))
        return carry

    lax.fori_loop(0, seq - 1, greet_seq, 0)
    lax.fori_loop(1, runs, greet_dp, 0)
    loads[0].wait()
    loads[1].wait()
    column = jnp.broadcast_to(mask[...].astype(jnp.float32), (tokens, tokens)).T.astype(jnp.bfloat16)
    for i in range(model // tokens):
        part = slice(i * tokens, (i + 1) * tokens)
        grads[d, :, part] = upstream[:, part] * column

    def turn(pair, carry):
        for c in range(3):
            at = pl.multiple_of(c * (heads * head) + pair * 2 * head, 2 * head)
            both = rows[:, pl.ds(at, 2 * head)].T
            turned[2 * pair, c] = both[:head]
            turned[2 * pair + 1, c] = both[head:]
        return carry

    loads[2].wait()
    lax.fori_loop(0, heads // 2, turn, 0)
    loads[3].wait()

    pl.semaphore_wait(barrier, seq - 1 + runs - 1)

    def weight_copy(at, k, peer):
        return pltpu.make_async_remote_copy(
            weight_rows(at), weight_rows(at), w_send.at[k], w_recv.at[at], **to(d, peer)
        )

    def weight_z(k, carry):
        weight_copy(s, k, (z + k) % 8 * 4 + y).start()
        return carry

    lax.fori_loop(1, 8, weight_z, 0)

    def grad_copy(run, k, peer):
        return pltpu.make_async_remote_copy(
            grads.at[run], grads.at[run], m_send.at[k], m_recv.at[run], **to(peer, s)
        )

    def chip(k):
        return (x + k) % 4 * 2

    def grads_x(k, carry):
        grad_copy(d, k, chip(k) + core).start()
        return carry

    lax.fori_loop(1, 4, grads_x, 0)
    grad_copy(d, 0, d + 1 - 2 * core).start()

    def qkv_copy(k):
        peer = shifted(z, y, k)
        return pltpu.make_async_remote_copy(
            turned.at[peer], qkv.at[s], q_send.at[k], q_recv.at[k], **to(d, peer)
        )

    def send_qkv(k, carry):
        qkv_copy(k).start()
        return carry

    lax.fori_loop(0, seq - 1, send_qkv, 0)
    qkv[s] = turned[s]

    def weight_y(k, carry):
        at = (z + k) % 8 * 4 + y

        @pl.when(k > 0)
        def _():
            weight_copy(at, 0, s).wait_recv()

        for i in range(1, 4):
            weight_copy(at, 8 * i + k, z * 4 + (y + i) % 4).start()
        return carry

    lax.fori_loop(0, 8, weight_y, 0)

    def weight_wait(k, carry):
        for i in range(1, 4):
            weight_copy(k * 4 + (y + i) % 4, 0, s).wait_recv()
        return carry

    lax.fori_loop(0, 8, weight_wait, 0)

    def sent_copy(run, source):
        return pltpu.make_async_remote_copy(
            sent.at[run], mixed.at[source], x_send.at[run], x_recv.at[source], **to(run, s)
        )

    def one_run(run):
        value = lax.dot_general(
            run_weight[...], grads[run], (((1,), (1,)), ((), ())), preferred_element_type=jnp.float32
        )
        sent[run] = value.astype(jnp.bfloat16).reshape(heads // runs, head, tokens)

        @pl.when(run != d)
        def _():
            sent_copy(run, d).start()

    def runs_near(k, carry):
        run = chip(k) + core

        @pl.when(k > 0)
        def _():
            grad_copy(run, 0, d).wait_recv()
            grad_copy(run, 3 + k, d + 1 - 2 * core).start()

        one_run(run)
        return carry

    lax.fori_loop(0, 4, runs_near, 0)

    def runs_other(k, carry):
        run = chip(k) + 1 - core
        grad_copy(run, 0, d).wait_recv()
        one_run(run)
        return carry

    lax.fori_loop(0, 4, runs_other, 0)

    mixed[d] = sent[d]

    def wait_mixed(k, carry):
        sent_copy(d, (d + k) % runs).wait_recv()
        return carry

    lax.fori_loop(1, runs, wait_mixed, 0)

    def head_copy(k):
        peer = shifted(z, y, k)
        share = heads // runs
        return pltpu.make_async_remote_copy(
            mixed.at[peer // share, peer % share], grad.at[s], g_send.at[k], g_recv.at[k], **to(d, peer)
        )

    def send_head(k, carry):
        head_copy(k).start()
        return carry

    lax.fori_loop(0, seq - 1, send_head, 0)
    grad[s] = mixed[s // (heads // runs), s % (heads // runs)]

    def finish_seq(k, carry):
        qkv_copy(k).wait()
        head_copy(k).wait()
        return carry

    lax.fori_loop(0, seq - 1, finish_seq, 0)

    def finish_sent(k, carry):
        sent_copy((d + k) % runs, d).wait_send()
        return carry

    lax.fori_loop(1, runs, finish_sent, 0)

    def finish_weight(k, carry):
        weight_copy(s, k, s).wait_send()
        return carry

    lax.fori_loop(1, 32, finish_weight, 0)

    def finish_grads(k, carry):
        grad_copy(d, k, d).wait_send()
        return carry

    lax.fori_loop(0, 7, finish_grads, 0)


def gather(weight, rows, upstream, mask, heads, runs):
    tokens, model = upstream.shape
    depth = weight.shape[0]
    vmem = pl.BlockSpec(memory_space=pltpu.VMEM)
    dma = pltpu.SemaphoreType.DMA
    return pl.pallas_call(
        gather_kernel,
        name="gather",
        out_shape=(
            jax.ShapeDtypeStruct((heads, 3, HS, tokens), jnp.bfloat16),
            jax.ShapeDtypeStruct((heads, HS, tokens), jnp.bfloat16),
            jax.ShapeDtypeStruct((runs, tokens, model), jnp.bfloat16),
            jax.ShapeDtypeStruct((heads * depth, model), jnp.bfloat16),
        ),
        in_specs=[pl.BlockSpec(memory_space=pltpu.HBM)] * 4,
        out_specs=(vmem,) * 4,
        scratch_shapes=[
            pltpu.VMEM(rows.shape, jnp.bfloat16),
            pltpu.VMEM(upstream.shape, jnp.bfloat16),
            pltpu.VMEM(mask.shape, jnp.int32),
            pltpu.VMEM((heads, 3, HS, tokens), jnp.bfloat16),
            pltpu.VMEM((runs, heads // runs, HS, tokens), jnp.bfloat16),
            pltpu.VMEM((runs, heads // runs, HS, tokens), jnp.bfloat16),
            dma((4,)),
            dma((heads,)),
            dma((heads,)),
            dma((8,)),
            dma((runs,)),
            dma((heads,)),
            dma((heads,)),
            dma((runs,)),
            dma((runs,)),
            dma((heads,)),
            dma((heads,)),
        ],
        cost_estimate=pl.CostEstimate(
            flops=2 * heads * depth * model * runs * tokens, bytes_accessed=16 << 20, transcendentals=0
        ),
        compiler_params=pltpu.CompilerParams(
            collective_id=0, has_side_effects=True, vmem_limit_bytes=24 << 20
        ),
    )(weight, rows, upstream, mask)


def scatter_kernel(
    results, grads, context, pieces, weight_grad,
    swapped, partial, across, along,
    c_send, c_recv, q_send, q_recv, s_send, s_recv, a_send, a_recv, l_send, l_recv,
):
    d, _, _, s, z, y = place()
    heads, _, head, tokens = results.shape
    runs, _, model = grads.shape
    group = heads // runs
    share = group * head
    depth = weight_grad.shape[0]

    def to(dp, at):
        return {"device_id": (dp, at), "device_id_type": MESH}

    barrier = pltpu.get_barrier_semaphore()

    def greet_seq(k, carry):
        pl.semaphore_signal(barrier, inc=1, **to(d, shifted(z, y, k)))
        return carry

    def greet_dp(k, carry):
        pl.semaphore_signal(barrier, inc=1, **to((d + k) % runs, s))
        return carry

    lax.fori_loop(0, heads - 1, greet_seq, 0)
    lax.fori_loop(1, runs, greet_dp, 0)
    pl.semaphore_wait(barrier, heads - 1 + runs - 1)

    def context_copy(k):
        peer = shifted(z, y, k)
        return pltpu.make_async_remote_copy(
            results.at[peer, 0], context.at[s], c_send.at[k], c_recv.at[k], **to(d, peer)
        )

    def piece_copy(k):
        peer = shifted(z, y, k)
        return pltpu.make_async_remote_copy(
            results.at[peer, pl.ds(1, 3)], pieces.at[:, s], q_send.at[k], q_recv.at[k], **to(d, peer)
        )

    def send_context(k, carry):
        context_copy(k).start()
        return carry

    def send_pieces(k, carry):
        piece_copy(k).start()
        return carry

    lax.fori_loop(0, heads - 1, send_context, 0)
    context[s] = results[s, 0]
    pieces[:, s] = results[s, 1:4]

    def wait_context(k, carry):
        context_copy(k).wait_recv()
        return carry

    lax.fori_loop(0, heads - 1, wait_context, 0)
    lax.fori_loop(0, heads - 1, send_pieces, 0)

    def swap_copy(k):
        peer = (d + k) % runs
        return pltpu.make_async_remote_copy(
            context.at[pl.ds(peer * group, group)], swapped.at[d], s_send.at[k], s_recv.at[k], **to(peer, s)
        )

    def send_swap(k, carry):
        swap_copy(k).start()
        return carry

    lax.fori_loop(1, runs, send_swap, 0)
    swapped[d] = context[pl.ds(d * group, group)]

    def wait_swap(k, carry):
        swap_copy(k).wait_recv()
        return carry

    lax.fori_loop(1, runs, wait_swap, 0)

    wide = 512

    def multiply(i, carry):
        at = pl.ds(pl.multiple_of(i * wide, wide), wide)
        left = jnp.concatenate([swapped[r].reshape(share, tokens) for r in range(runs)], 1)
        right = grads[:, :, at].reshape(runs * tokens, wide)
        total = jnp.dot(left, right, preferred_element_type=jnp.float32).astype(jnp.bfloat16)
        for k in range(heads):
            partial[k % 4, k // 4, :, at] = total[k * depth : (k + 1) * depth]
        return carry

    lax.fori_loop(0, model // wide, multiply, 0)

    def across_copy(k):
        peer = (y + k) % 4
        return pltpu.make_async_remote_copy(
            partial.at[peer], across.at[k], a_send.at[k], a_recv.at[k], **to(d, z * 4 + peer)
        )

    for k in range(1, 4):
        across_copy(k).start()

    for k in range(1, 4):
        across_copy(k).wait_recv()

    def add_across(k, carry):
        total = partial[y, k].astype(jnp.float32)
        for i in range(1, 4):
            total += across[i, k].astype(jnp.float32)
        across[0, k] = total.astype(jnp.bfloat16)
        return carry

    def along_copy(k):
        peer = (z + k) % 8
        return pltpu.make_async_remote_copy(
            across.at[0, peer], along.at[k], l_send.at[k], l_recv.at[k], **to(d, peer * 4 + y)
        )

    def send_along(k, carry):
        along_copy(k).start()
        return carry

    lax.fori_loop(0, 8, add_across, 0)
    lax.fori_loop(1, 8, send_along, 0)

    def wait_pieces(k, carry):
        piece_copy(k).wait_recv()
        return carry

    def wait_along(k, carry):
        along_copy(k).wait_recv()
        return carry

    lax.fori_loop(1, 8, wait_along, 0)
    total = across[0, z].astype(jnp.float32)
    for k in range(1, 8):
        total += along[k].astype(jnp.float32)
    weight_grad[...] = total
    lax.fori_loop(0, heads - 1, wait_pieces, 0)

    def finish_seq(k, carry):
        context_copy(k).wait_send()
        piece_copy(k).wait_send()
        return carry

    def finish_swap(k, carry):
        swap_copy(k).wait_send()
        return carry

    def finish_along(k, carry):
        along_copy(k).wait_send()
        return carry

    lax.fori_loop(0, heads - 1, finish_seq, 0)
    lax.fori_loop(1, runs, finish_swap, 0)
    for k in range(1, 4):
        across_copy(k).wait_send()
    lax.fori_loop(1, 8, finish_along, 0)


def scatter(results, grads, depth):
    heads, _, head, tokens = results.shape
    runs, _, model = grads.shape
    bf16, dma = jnp.bfloat16, pltpu.SemaphoreType.DMA
    vmem = pl.BlockSpec(memory_space=pltpu.VMEM)
    return pl.pallas_call(
        scatter_kernel,
        name="scatter",
        out_shape=(
            jax.ShapeDtypeStruct((heads, head, tokens), bf16),
            jax.ShapeDtypeStruct((3, heads, head, tokens), bf16),
            jax.ShapeDtypeStruct((depth, model), jnp.float32),
        ),
        in_specs=[vmem] * 2,
        out_specs=(vmem,) * 3,
        scratch_shapes=[
            pltpu.VMEM((runs, heads // runs, head, tokens), bf16),
            pltpu.VMEM((4, 8, depth, model), bf16),
            pltpu.VMEM((4, 8, depth, model), bf16),
            pltpu.VMEM((8, depth, model), bf16),
            dma((heads,)), dma((heads,)), dma((heads,)), dma((heads,)),
            dma((runs,)), dma((runs,)), dma((4,)), dma((4,)), dma((8,)), dma((8,)),
        ],
        cost_estimate=pl.CostEstimate(
            flops=2 * heads * head * model * tokens, bytes_accessed=20 << 20, transcendentals=0
        ),
        compiler_params=pltpu.CompilerParams(
            collective_id=1, has_side_effects=True, vmem_limit_bytes=24 << 20
        ),
    )(results, grads)


def on_device(projected, out_weight, upstream, peak_mask, block_layout):
    inner = projected.shape[2] // 3
    heads = inner // HS
    dp = lax.axis_size("dp")

    qkv, grad_heads, run_grads, run_weight = gather(
        out_weight, projected[0], upstream[0], peak_mask, heads, dp
    )
    full_weight = lax.all_gather(run_weight, "dp", axis=0, tiled=True)
    results = attention(block_layout[0], qkv, grad_heads)
    context, projected_grad, weight_grad = scatter(results, run_grads, out_weight.shape[0])
    attended = lax.dot_general(
        context.reshape(inner, -1),
        full_weight,
        (((0,), (0,)), ((), ())),
        preferred_element_type=jnp.float32,
    ).astype(jnp.bfloat16)
    projected_grad = projected_grad.reshape(3 * inner, -1).T
    return (attended[None], projected_grad[None], weight_grad)


def solution(mesh):
    in_specs = (
        P("dp", "seq", None),
        P(("dp", "seq"), None),
        P("dp", "seq", None),
        P("dp", "seq"),
        P("seq", None, None),
    )
    out_specs = (P("dp", "seq", None), P("dp", "seq", None), P(("dp", "seq"), None))
    return jax.shard_map(
        on_device, mesh=mesh, in_specs=in_specs, out_specs=out_specs, check_vma=False
    )
```

```python
import jax
import jax.numpy as jnp
from jax import lax
from jax.experimental import pallas as pl
from jax.experimental.pallas import tpu as pltpu
from jax.sharding import PartitionSpec as P

HS = 64
SCALE = 0.125


MESH = pl.DeviceIdType.MESH


def place():
    d, s = lax.axis_index("dp"), lax.axis_index("seq")
    return d, d // 2, d % 2, s, s // 4, s % 4


def shifted(z, y, k):
    along, across = k // 4, k % 4
    along = 4 + (1 - along % 2 * 2) * ((along + 1) // 2)
    across = 2 + (1 - across % 2 * 2) * ((across + 1) // 2)
    return (z + along) % 8 * 4 + (y + across) % 4


def layer_kernel(
    layout, where, weight, rows_in, upstream_in, mask_in, attended, pieces, weight_grad,
    qkv, grad, grads, run_weight, rows, upstream, mask, turned, sent, mixed, full_weight,
    kvn, parts, probs, scores, out, context, swapped, partial, across, along,
    in_sem, w_send, w_recv, m_send, m_recv, q_send, q_recv, x_send, x_recv, g_send, g_recv,
    f_send, f_recv, c_send, c_recv, b_send, b_recv, k_send, k_recv,
    s_send, s_recv, a_send, a_recv, l_send, l_recv,
):
    d, x, core, s, z, y = place()
    tokens, model = upstream.shape
    heads, _, head, _ = qkv.shape
    seq, runs, depth = heads, grads.shape[0], weight.shape[0]
    group = heads // runs
    share = group * head
    other = d + 1 - 2 * core

    def to(dp, at):
        return {"device_id": (dp, at), "device_id_type": MESH}

    def weight_rows(at):
        return run_weight.at[pl.ds(pl.multiple_of(at * depth, depth), depth)]

    loads = [
        pltpu.make_async_copy(upstream_in, upstream, in_sem.at[0]),
        pltpu.make_async_copy(mask_in, mask, in_sem.at[1]),
        pltpu.make_async_copy(rows_in, rows, in_sem.at[2]),
        pltpu.make_async_copy(weight, weight_rows(s), in_sem.at[3]),
    ]
    for load in loads:
        load.start()
    barrier = pltpu.get_barrier_semaphore()

    def greet_seq(k, carry):
        pl.semaphore_signal(barrier, inc=1, **to(d, shifted(z, y, k)))
        return carry

    def greet_dp(k, carry):
        pl.semaphore_signal(barrier, inc=1, **to((d + k) % runs, s))
        return carry

    lax.fori_loop(0, seq - 1, greet_seq, 0)
    lax.fori_loop(1, runs, greet_dp, 0)
    loads[0].wait()
    loads[1].wait()
    column = jnp.broadcast_to(mask[...].astype(jnp.float32), (tokens, tokens)).T.astype(jnp.bfloat16)
    for i in range(model // tokens):
        part = slice(i * tokens, (i + 1) * tokens)
        grads[d, :, part] = upstream[:, part] * column

    def turn(pair, carry):
        for c in range(3):
            at = pl.multiple_of(c * (heads * head) + pair * 2 * head, 2 * head)
            both = rows[:, pl.ds(at, 2 * head)].T
            turned[2 * pair, c] = both[:head]
            turned[2 * pair + 1, c] = both[head:]
        return carry

    loads[2].wait()
    lax.fori_loop(0, heads // 2, turn, 0)
    loads[3].wait()

    pl.semaphore_wait(barrier, seq - 1 + runs - 1)

    def weight_copy(at, k, peer):
        return pltpu.make_async_remote_copy(
            weight_rows(at), weight_rows(at), w_send.at[k], w_recv.at[at], **to(d, peer)
        )

    def weight_z(k, carry):
        weight_copy(s, k, (z + k) % 8 * 4 + y).start()
        return carry

    lax.fori_loop(1, 8, weight_z, 0)

    def grad_copy(run, k, peer):
        return pltpu.make_async_remote_copy(
            grads.at[run], grads.at[run], m_send.at[k], m_recv.at[run], **to(peer, s)
        )

    def chip(k):
        return (x + k) % 4 * 2

    def grads_x(k, carry):
        grad_copy(d, k, chip(k) + core).start()
        return carry

    lax.fori_loop(1, 4, grads_x, 0)
    grad_copy(d, 0, d + 1 - 2 * core).start()

    def qkv_copy(k):
        peer = shifted(z, y, k)
        return pltpu.make_async_remote_copy(
            turned.at[peer], qkv.at[s], q_send.at[k], q_recv.at[k], **to(d, peer)
        )

    def send_qkv(k, carry):
        qkv_copy(k).start()
        return carry

    lax.fori_loop(0, seq - 1, send_qkv, 0)
    qkv[s] = turned[s]

    def weight_y(k, carry):
        at = (z + k) % 8 * 4 + y

        @pl.when(k > 0)
        def _():
            weight_copy(at, 0, s).wait_recv()

        for i in range(1, 4):
            weight_copy(at, 8 * i + k, z * 4 + (y + i) % 4).start()
        return carry

    lax.fori_loop(0, 8, weight_y, 0)

    def weight_wait(k, carry):
        for i in range(1, 4):
            weight_copy(k * 4 + (y + i) % 4, 0, s).wait_recv()
        return carry

    lax.fori_loop(0, 8, weight_wait, 0)

    def sent_copy(run, source):
        return pltpu.make_async_remote_copy(
            sent.at[run], mixed.at[source], x_send.at[run], x_recv.at[source], **to(run, s)
        )

    def one_run(run):
        value = lax.dot_general(
            run_weight[...], grads[run], (((1,), (1,)), ((), ())), preferred_element_type=jnp.float32
        )
        sent[run] = value.astype(jnp.bfloat16).reshape(heads // runs, head, tokens)

        @pl.when(run != d)
        def _():
            sent_copy(run, d).start()

    def runs_near(k, carry):
        run = chip(k) + core

        @pl.when(k > 0)
        def _():
            grad_copy(run, 0, d).wait_recv()
            grad_copy(run, 3 + k, d + 1 - 2 * core).start()

        one_run(run)
        return carry

    lax.fori_loop(0, 4, runs_near, 0)

    def runs_other(k, carry):
        run = chip(k) + 1 - core
        grad_copy(run, 0, d).wait_recv()
        one_run(run)
        return carry

    lax.fori_loop(0, 4, runs_other, 0)

    mixed[d] = sent[d]

    def full_copy(run, k, peer):
        source = run_weight if run is d else full_weight.at[run]
        return pltpu.make_async_remote_copy(
            source, full_weight.at[run], f_send.at[k], f_recv.at[run], **to(peer, s)
        )

    def full_x(k, carry):
        full_copy(d, k, chip(k) + core).start()
        return carry

    lax.fori_loop(1, 4, full_x, 0)
    full_copy(d, 0, other).start()

    def wait_mixed(k, carry):
        sent_copy(d, (d + k) % runs).wait_recv()
        return carry

    lax.fori_loop(1, runs, wait_mixed, 0)

    def head_copy(k):
        peer = shifted(z, y, k)
        return pltpu.make_async_remote_copy(
            mixed.at[peer // group, peer % group], grad.at[s], g_send.at[k], g_recv.at[k], **to(d, peer)
        )

    def send_head(k, carry):
        head_copy(k).start()
        return carry

    lax.fori_loop(0, seq - 1, send_head, 0)
    grad[s] = mixed[s // (heads // runs), s % (heads // runs)]

    def arrive_qkv(k, carry):
        qkv_copy(k).wait_recv()
        return carry

    lax.fori_loop(0, seq - 1, arrive_qkv, 0)

    blocks, length = heads, tokens
    picks = layout.shape[1]
    pair = 2 * head
    eighths = length // 8

    def prepare(b, carry):
        kvn[b] = qkv[b, 1:3].reshape(pair, length).T
        return carry

    lax.fori_loop(0, blocks, prepare, 0, unroll=4)
    parts[blocks * picks] = jnp.zeros((length, pair), jnp.float32)

    def arrive_grad(k, carry):
        head_copy(k).wait_recv()
        return carry

    lax.fori_loop(0, seq - 1, arrive_grad, 0)
    low = lax.broadcasted_iota(jnp.int32, (length, pair), 1) < head

    def picked(r):
        return [layout[r, j] for j in range(picks)]

    def scores_of(r, slot):
        q = qkv[r, 0] * jnp.bfloat16(SCALE)
        g = grad[r]
        none = jnp.zeros_like(q)
        into = jnp.concatenate([jnp.concatenate([q, none], 1), jnp.concatenate([none, g], 1)], 0)
        top = None
        for j, b in enumerate(picked(r)):
            both = jnp.dot(kvn[b], into, preferred_element_type=jnp.float32)
            scores[slot, j] = both
            part = jnp.max(both[:, :length].reshape(eighths, 8, length), axis=0)
            top = part if top is None else jnp.maximum(top, part)
        return jnp.max(top, axis=0, keepdims=True)

    def probs_of(slot, top):
        total = jnp.zeros((8, length), jnp.float32)
        delta = jnp.zeros((8, length), jnp.float32)
        for j in range(picks):
            e = jnp.exp(scores[slot, j, :, :length] - top)
            scores[slot, j, :, :length] = e
            total += jnp.sum(e.reshape(eighths, 8, length), axis=0)
            delta += jnp.sum((e * scores[slot, j, :, length:]).reshape(eighths, 8, length), axis=0)
        inverse = 1.0 / jnp.sum(total, axis=0, keepdims=True)
        delta = jnp.sum(delta, axis=0, keepdims=True) * inverse
        for j in range(picks):
            p = scores[slot, j, :, :length] * inverse
            d = p * (scores[slot, j, :, length:] - delta)
            rows = pl.ds(j * length, length)
            probs[slot, rows, :length] = d.astype(jnp.bfloat16)
            probs[slot, rows, length:] = p.astype(jnp.bfloat16)

    def results_of(r, slot):
        at = picked(r)
        kvt = jnp.concatenate([qkv[b, 1:3].reshape(pair, length) for b in at], 1)
        both = jnp.dot(kvt, probs[slot], preferred_element_type=jnp.float32)
        out[r, 0] = both[head:, length:].astype(jnp.bfloat16)
        out[r, 1] = (both[:head, :length] * SCALE).astype(jnp.bfloat16)
        turned = jnp.concatenate([qkv[r, 0] * jnp.bfloat16(SCALE), grad[r]], 0).T
        into = jnp.concatenate([jnp.where(low, turned, 0), jnp.where(low, 0, turned)], 0)
        for j in range(picks):
            parts[r * picks + j] = jnp.dot(
                probs[slot, pl.ds(j * length, length), :], into, preferred_element_type=jnp.float32
            )

    def context_copy(k):
        peer = shifted(z, y, k)
        return pltpu.make_async_remote_copy(
            out.at[peer, 0], context.at[s], c_send.at[k], c_recv.at[k], **to(d, peer)
        )

    def query_copy(k):
        peer = shifted(z, y, k)
        return pltpu.make_async_remote_copy(
            out.at[peer, 1], pieces.at[0, s], b_send.at[k], b_recv.at[k], **to(d, peer)
        )

    def key_copy(k):
        peer = shifted(z, y, k)
        return pltpu.make_async_remote_copy(
            out.at[peer, pl.ds(2, 2)], pieces.at[pl.ds(1, 2), s], k_send.at[k], k_recv.at[k], **to(d, peer)
        )

    def row(k):
        return shifted(z, y, k)

    def give(k, slot):
        results_of(row(k), slot)
        context_copy(k).start()
        query_copy(k).start()

    probs_of(0, scores_of(row(0), 0))

    def two_rows(i, top):
        k = 2 * i
        later = scores_of(row(k + 2), 0)
        give(k, 0)
        probs_of(1, top)
        last = scores_of(row(k + 3), 1)
        give(k + 1, 1)
        probs_of(0, later)
        return last

    top = lax.fori_loop(0, blocks // 2 - 1, two_rows, scores_of(row(1), 1))
    give(blocks - 2, 0)
    probs_of(1, top)
    results_of(s, 1)
    context[s] = out[s, 0]
    pieces[0, s] = out[s, 1]

    def wait_context(k, carry):
        context_copy(k).wait_recv()
        return carry

    lax.fori_loop(0, seq - 1, wait_context, 0)

    def swap_copy(k):
        peer = (d + k) % runs
        return pltpu.make_async_remote_copy(
            context.at[pl.ds(peer * group, group)], swapped.at[d], s_send.at[k], s_recv.at[k], **to(peer, s)
        )

    def send_swap(k, carry):
        swap_copy(k).start()
        return carry

    lax.fori_loop(1, runs, send_swap, 0)
    swapped[d] = context[pl.ds(d * group, group)]

    def keys_of(u):
        total = parts[where[u, 0]]
        for r in range(1, blocks):
            total += parts[where[u, r]]
        out[u, 2:4] = total.T.astype(jnp.bfloat16).reshape(2, head, length)

    def give_keys(k, carry):
        keys_of(row(k))
        key_copy(k).start()
        return carry

    lax.fori_loop(0, seq - 1, give_keys, 0)
    keys_of(s)
    pieces[1:3, s] = out[s, 2:4]

    def wait_swap(k, carry):
        swap_copy(k).wait_recv()
        return carry

    lax.fori_loop(1, runs, wait_swap, 0)

    wide = 512

    def multiply(i, carry):
        at = pl.ds(pl.multiple_of(i * wide, wide), wide)
        left = jnp.concatenate([swapped[r].reshape(share, tokens) for r in range(runs)], 1)
        right = grads[:, :, at].reshape(runs * tokens, wide)
        total = jnp.dot(left, right, preferred_element_type=jnp.float32).astype(jnp.bfloat16)
        for k in range(heads):
            partial[k % 4, k // 4, :, at] = total[k * depth : (k + 1) * depth]
        return carry

    lax.fori_loop(0, model // wide, multiply, 0)

    def across_copy(k):
        peer = (y + k) % 4
        return pltpu.make_async_remote_copy(
            partial.at[peer], across.at[k], a_send.at[k], a_recv.at[k], **to(d, z * 4 + peer)
        )

    for k in range(1, 4):
        across_copy(k).start()

    def attend(run, rows):
        left = context[pl.ds(run * group, group)].reshape(share, tokens).T
        return jnp.dot(left, rows, preferred_element_type=jnp.float32)

    def full_near(k, carry):
        run = chip(k) + core
        full_copy(run, 0, d).wait_recv()
        full_copy(run, 3 + k, other).start()
        attended[...] += attend(run, full_weight[run])
        return carry

    def full_other(k, carry):
        run = chip(k) + 1 - core
        full_copy(run, 0, d).wait_recv()
        attended[...] += attend(run, full_weight[run])
        return carry

    attended[...] = attend(d, run_weight[...])
    lax.fori_loop(1, 4, full_near, 0)

    for k in range(1, 4):
        across_copy(k).wait_recv()

    def add_across(k, carry):
        total = partial[y, k].astype(jnp.float32)
        for i in range(1, 4):
            total += across[i, k].astype(jnp.float32)
        across[0, k] = total.astype(jnp.bfloat16)
        return carry

    def along_copy(k):
        peer = (z + k) % 8
        return pltpu.make_async_remote_copy(
            across.at[0, peer], along.at[k], l_send.at[k], l_recv.at[k], **to(d, peer * 4 + y)
        )

    def send_along(k, carry):
        along_copy(k).start()
        return carry

    lax.fori_loop(0, 8, add_across, 0)
    lax.fori_loop(1, 8, send_along, 0)
    lax.fori_loop(0, 4, full_other, 0)

    def wait_along(k, carry):
        along_copy(k).wait_recv()
        return carry

    lax.fori_loop(1, 8, wait_along, 0)
    total = across[0, z].astype(jnp.float32)
    for k in range(1, 8):
        total += along[k].astype(jnp.float32)
    weight_grad[...] = total

    def finish_seq(k, carry):
        qkv_copy(k).wait_send()
        head_copy(k).wait_send()
        context_copy(k).wait_send()
        query_copy(k).wait()
        key_copy(k).wait()
        return carry

    lax.fori_loop(0, seq - 1, finish_seq, 0)

    def finish_swap(k, carry):
        swap_copy(k).wait_send()
        return carry

    def finish_along(k, carry):
        along_copy(k).wait_send()
        return carry

    lax.fori_loop(1, runs, finish_swap, 0)
    for k in range(1, 4):
        across_copy(k).wait_send()
    lax.fori_loop(1, 8, finish_along, 0)

    def finish_sent(k, carry):
        sent_copy((d + k) % runs, d).wait_send()
        return carry

    lax.fori_loop(1, runs, finish_sent, 0)

    def finish_weight(k, carry):
        weight_copy(s, k, s).wait_send()
        return carry

    lax.fori_loop(1, 32, finish_weight, 0)

    def finish_grads(k, carry):
        grad_copy(d, k, d).wait_send()
        return carry

    lax.fori_loop(0, 7, finish_grads, 0)

    def finish_full(k, carry):
        full_copy(d, k, other).wait_send()
        return carry

    lax.fori_loop(0, 7, finish_full, 0)


def layer(layout, where, weight, rows, upstream, mask, runs):
    tokens, model = upstream.shape
    heads, picks = layout.shape
    depth = weight.shape[0]
    group = heads // runs
    bf16, f32, dma = jnp.bfloat16, jnp.float32, pltpu.SemaphoreType.DMA
    vmem, smem = pl.BlockSpec(memory_space=pltpu.VMEM), pl.BlockSpec(memory_space=pltpu.SMEM)
    each, some = dma((heads,)), dma((8,))
    return pl.pallas_call(
        layer_kernel,
        name="layer",
        out_shape=(
            jax.ShapeDtypeStruct((tokens, model), f32),
            jax.ShapeDtypeStruct((3, heads, HS, tokens), bf16),
            jax.ShapeDtypeStruct((depth, model), f32),
        ),
        in_specs=[smem, smem] + [pl.BlockSpec(memory_space=pltpu.HBM)] * 4,
        out_specs=(vmem,) * 3,
        scratch_shapes=[
            pltpu.VMEM((heads, 3, HS, tokens), bf16),
            pltpu.VMEM((heads, HS, tokens), bf16),
            pltpu.VMEM((runs, tokens, model), bf16),
            pltpu.VMEM((heads * depth, model), bf16),
            pltpu.VMEM(rows.shape, bf16),
            pltpu.VMEM(upstream.shape, bf16),
            pltpu.VMEM(mask.shape, jnp.int32),
            pltpu.VMEM((heads, 3, HS, tokens), bf16),
            pltpu.VMEM((runs, group, HS, tokens), bf16),
            pltpu.VMEM((runs, group, HS, tokens), bf16),
            pltpu.VMEM((runs, heads * depth, model), bf16),
            pltpu.VMEM((heads, tokens, 2 * HS), bf16),
            pltpu.VMEM((heads * picks + 1, tokens, 2 * HS), f32),
            pltpu.VMEM((2, picks * tokens, 2 * tokens), bf16),
            pltpu.VMEM((2, picks, tokens, 2 * tokens), f32),
            pltpu.VMEM((heads, 4, HS, tokens), bf16),
            pltpu.VMEM((heads, HS, tokens), bf16),
            pltpu.VMEM((runs, group, HS, tokens), bf16),
            pltpu.VMEM((4, 8, depth, model), bf16),
            pltpu.VMEM((4, 8, depth, model), bf16),
            pltpu.VMEM((8, depth, model), bf16),
            dma((4,)), each, each, some, some, each, each, some, some, each, each,
            some, some, each, each, each, each, each, each,
            some, some, dma((4,)), dma((4,)), some, some,
        ],
        cost_estimate=pl.CostEstimate(
            flops=20 * heads * tokens * picks * tokens * HS, bytes_accessed=16 << 20, transcendentals=0
        ),
        compiler_params=pltpu.CompilerParams(
            collective_id=0, has_side_effects=True, vmem_limit_bytes=58 << 20
        ),
    )(layout, where, weight, rows, upstream, mask)


def on_device(projected, out_weight, upstream, peak_mask, block_layout):
    inner = projected.shape[2] // 3
    layout = block_layout[0]
    blocks, picks = layout.shape
    index = jnp.arange(blocks * picks, dtype=jnp.int32).reshape(1, blocks, picks)
    same = layout[None] == jnp.arange(blocks, dtype=jnp.int32)[:, None, None]
    where = jnp.min(jnp.where(same, index, blocks * picks), axis=2)
    attended, projected_grad, weight_grad = layer(
        layout, where, out_weight, projected[0], upstream[0], peak_mask, lax.axis_size("dp")
    )
    projected_grad = projected_grad.reshape(3 * inner, -1).T
    return (attended.astype(jnp.bfloat16)[None], projected_grad[None], weight_grad)


def solution(mesh):
    in_specs = (
        P("dp", "seq", None),
        P(("dp", "seq"), None),
        P("dp", "seq", None),
        P("dp", "seq"),
        P("seq", None, None),
    )
    out_specs = (P("dp", "seq", None), P("dp", "seq", None), P(("dp", "seq"), None))
    return jax.shard_map(
        on_device, mesh=mesh, in_specs=in_specs, out_specs=out_specs, check_vma=False
    )
```

```python
import jax
import jax.numpy as jnp
from jax import lax
from jax.experimental import pallas as pl
from jax.experimental.pallas import tpu as pltpu
from jax.sharding import PartitionSpec as P

HS = 64
SCALE = 0.125


MESH = pl.DeviceIdType.MESH


def place():
    d, s = lax.axis_index("dp"), lax.axis_index("seq")
    return d, d // 2, d % 2, s, s // 4, s % 4


def shifted(z, y, k):
    along, across = k // 4, k % 4
    along = 4 + (1 - along % 2 * 2) * ((along + 1) // 2)
    across = 2 + (1 - across % 2 * 2) * ((across + 1) // 2)
    return (z + along) % 8 * 4 + (y + across) % 4


def layer_kernel(
    layout, where, weight, rows_in, upstream_in, mask_in, attended, pieces, weight_grad,
    qkv, grad, grads, run_weight, rows, upstream, mask, turned, sent, mixed, full_weight,
    kvn, parts, probs, slopes, scores, out, context, swapped, partial, across, along,
    in_sem, w_send, w_recv, m_send, m_recv, q_send, q_recv, x_send, x_recv, g_send, g_recv,
    f_send, f_recv, c_send, c_recv, b_send, b_recv, k_send, k_recv,
    s_send, s_recv, a_send, a_recv, l_send, l_recv,
):
    d, x, core, s, z, y = place()
    tokens, model = upstream.shape
    heads, _, head, _ = qkv.shape
    seq, runs, depth = heads, grads.shape[0], weight.shape[0]
    group = heads // runs
    share = group * head
    other = d + 1 - 2 * core

    def to(dp, at):
        return {"device_id": (dp, at), "device_id_type": MESH}

    def weight_rows(at):
        return run_weight.at[pl.ds(pl.multiple_of(at * depth, depth), depth)]

    loads = [
        pltpu.make_async_copy(upstream_in, upstream, in_sem.at[0]),
        pltpu.make_async_copy(mask_in, mask, in_sem.at[1]),
        pltpu.make_async_copy(rows_in, rows, in_sem.at[2]),
        pltpu.make_async_copy(weight, weight_rows(s), in_sem.at[3]),
    ]
    for load in loads:
        load.start()
    barrier = pltpu.get_barrier_semaphore()

    def greet_seq(k, carry):
        pl.semaphore_signal(barrier, inc=1, **to(d, shifted(z, y, k)))
        return carry

    def greet_dp(k, carry):
        pl.semaphore_signal(barrier, inc=1, **to((d + k) % runs, s))
        return carry

    lax.fori_loop(0, seq - 1, greet_seq, 0)
    lax.fori_loop(1, runs, greet_dp, 0)
    loads[0].wait()
    loads[1].wait()
    column = jnp.broadcast_to(mask[...].astype(jnp.float32), (tokens, tokens)).T.astype(jnp.bfloat16)
    for i in range(model // tokens):
        part = slice(i * tokens, (i + 1) * tokens)
        grads[d, :, part] = upstream[:, part] * column

    def turn(pair, carry):
        for c in range(3):
            at = pl.multiple_of(c * (heads * head) + pair * 2 * head, 2 * head)
            both = rows[:, pl.ds(at, 2 * head)].T
            turned[2 * pair, c] = both[:head]
            turned[2 * pair + 1, c] = both[head:]
        return carry

    loads[2].wait()
    lax.fori_loop(0, heads // 2, turn, 0)
    loads[3].wait()

    pl.semaphore_wait(barrier, seq - 1 + runs - 1)

    def weight_copy(at, k, peer):
        return pltpu.make_async_remote_copy(
            weight_rows(at), weight_rows(at), w_send.at[k], w_recv.at[at], **to(d, peer)
        )

    def weight_z(k, carry):
        weight_copy(s, k, (z + k) % 8 * 4 + y).start()
        return carry

    lax.fori_loop(1, 8, weight_z, 0)

    def grad_copy(run, k, peer):
        return pltpu.make_async_remote_copy(
            grads.at[run], grads.at[run], m_send.at[k], m_recv.at[run], **to(peer, s)
        )

    def chip(k):
        return (x + k) % 4 * 2

    def grads_x(k, carry):
        grad_copy(d, k, chip(k) + core).start()
        return carry

    lax.fori_loop(1, 4, grads_x, 0)
    grad_copy(d, 0, d + 1 - 2 * core).start()

    def qkv_copy(k):
        peer = shifted(z, y, k)
        return pltpu.make_async_remote_copy(
            turned.at[peer], qkv.at[s], q_send.at[k], q_recv.at[k], **to(d, peer)
        )

    def send_qkv(k, carry):
        qkv_copy(k).start()
        return carry

    lax.fori_loop(0, seq - 1, send_qkv, 0)
    qkv[s] = turned[s]

    def weight_y(k, carry):
        at = (z + k) % 8 * 4 + y

        @pl.when(k > 0)
        def _():
            weight_copy(at, 0, s).wait_recv()

        for i in range(1, 4):
            weight_copy(at, 8 * i + k, z * 4 + (y + i) % 4).start()
        return carry

    lax.fori_loop(0, 8, weight_y, 0)

    def weight_wait(k, carry):
        for i in range(1, 4):
            weight_copy(k * 4 + (y + i) % 4, 0, s).wait_recv()
        return carry

    lax.fori_loop(0, 8, weight_wait, 0)

    def sent_copy(run, source):
        return pltpu.make_async_remote_copy(
            sent.at[run], mixed.at[source], x_send.at[run], x_recv.at[source], **to(run, s)
        )

    def one_run(run):
        value = lax.dot_general(
            run_weight[...], grads[run], (((1,), (1,)), ((), ())), preferred_element_type=jnp.float32
        )
        sent[run] = value.astype(jnp.bfloat16).reshape(heads // runs, head, tokens)

        @pl.when(run != d)
        def _():
            sent_copy(run, d).start()

    def runs_near(k, carry):
        run = chip(k) + core

        @pl.when(k > 0)
        def _():
            grad_copy(run, 0, d).wait_recv()
            grad_copy(run, 3 + k, d + 1 - 2 * core).start()

        one_run(run)
        return carry

    lax.fori_loop(0, 4, runs_near, 0)

    def runs_other(k, carry):
        run = chip(k) + 1 - core
        grad_copy(run, 0, d).wait_recv()
        one_run(run)
        return carry

    lax.fori_loop(0, 4, runs_other, 0)

    mixed[d] = sent[d]

    def full_copy(run, k, peer):
        source = run_weight if run is d else full_weight.at[run]
        return pltpu.make_async_remote_copy(
            source, full_weight.at[run], f_send.at[k], f_recv.at[run], **to(peer, s)
        )

    def full_x(k, carry):
        full_copy(d, k, chip(k) + core).start()
        return carry

    lax.fori_loop(1, 4, full_x, 0)
    full_copy(d, 0, other).start()

    def wait_mixed(k, carry):
        sent_copy(d, (d + k) % runs).wait_recv()
        return carry

    lax.fori_loop(1, runs, wait_mixed, 0)

    def head_copy(k):
        peer = shifted(z, y, k)
        return pltpu.make_async_remote_copy(
            mixed.at[peer // group, peer % group], grad.at[s], g_send.at[k], g_recv.at[k], **to(d, peer)
        )

    def send_head(k, carry):
        head_copy(k).start()
        return carry

    lax.fori_loop(0, seq - 1, send_head, 0)
    grad[s] = mixed[s // (heads // runs), s % (heads // runs)]

    def arrive_qkv(k, carry):
        qkv_copy(k).wait_recv()
        return carry

    lax.fori_loop(0, seq - 1, arrive_qkv, 0)

    blocks, length = heads, tokens
    picks = layout.shape[0]
    pair = 2 * head
    eighths = length // 8

    def prepare(b, carry):
        kvn[b] = qkv[b, 1:3].reshape(pair, length).T
        return carry

    lax.fori_loop(0, blocks, prepare, 0, unroll=4)
    parts[blocks * picks] = jnp.zeros((length, pair), jnp.float32)

    low = lax.broadcasted_iota(jnp.int32, (length, pair), 1) < head

    def picked(r):
        return [layout[j, r] for j in range(picks)]

    def row(k):
        return shifted(z, y, k)

    def scores_of(k, slot):
        q = qkv[row(k), 0] * jnp.bfloat16(SCALE)
        into = jnp.concatenate([q, jnp.zeros_like(q)], 0)
        top = None
        for j, b in enumerate(picked(row(k))):
            score = jnp.dot(kvn[b], into, preferred_element_type=jnp.float32)
            scores[slot, j] = score
            part = jnp.max(score.reshape(eighths, 8, length), axis=0)
            top = part if top is None else jnp.maximum(top, part)
        return jnp.max(top, axis=0, keepdims=True)

    def probs_of(k, slot, top):
        total = jnp.zeros((8, length), jnp.float32)
        for j in range(picks):
            e = jnp.exp(scores[slot, j] - top)
            scores[slot, j] = e
            total += jnp.sum(e.reshape(eighths, 8, length), axis=0)
        inverse = 1.0 / jnp.sum(total, axis=0, keepdims=True)
        for j in range(picks):
            probs[k, pl.ds(j * length, length)] = (scores[slot, j] * inverse).astype(jnp.bfloat16)

    def context_of(k):
        values = jnp.concatenate([qkv[b, 2] for b in picked(row(k))], 1)
        out[row(k), 0] = jnp.dot(
            values, probs[k], preferred_element_type=jnp.float32
        ).astype(jnp.bfloat16)

    def slopes_of(k, slot):
        g = grad[row(k)]
        into = jnp.concatenate([jnp.zeros_like(g), g], 0)
        delta = jnp.sum(
            g.astype(jnp.float32) * out[row(k), 0].astype(jnp.float32), axis=0, keepdims=True
        )
        for j, b in enumerate(picked(row(k))):
            rows = pl.ds(j * length, length)
            slope = jnp.dot(kvn[b], into, preferred_element_type=jnp.float32) - delta
            slope = probs[k, rows].astype(jnp.float32) * slope
            slopes[slot, rows] = slope.astype(jnp.bfloat16)

    def results_of(k, slot):
        r = row(k)
        keys = jnp.concatenate([qkv[b, 1] for b in picked(r)], 1)
        value = jnp.dot(keys, slopes[slot], preferred_element_type=jnp.float32)
        out[r, 1] = (value * SCALE).astype(jnp.bfloat16)
        turned = jnp.concatenate([qkv[r, 0] * jnp.bfloat16(SCALE), grad[r]], 0).T
        into = jnp.concatenate([jnp.where(low, turned, 0), jnp.where(low, 0, turned)], 0)
        for j in range(picks):
            rows = pl.ds(j * length, length)
            both = jnp.concatenate([slopes[slot, rows], probs[k, rows]], 1)
            parts[r * picks + j] = jnp.dot(both, into, preferred_element_type=jnp.float32)

    def context_copy(k):
        peer = shifted(z, y, k)
        return pltpu.make_async_remote_copy(
            out.at[peer, 0], context.at[s], c_send.at[k], c_recv.at[k], **to(d, peer)
        )

    def query_copy(k):
        peer = shifted(z, y, k)
        return pltpu.make_async_remote_copy(
            out.at[peer, 1], pieces.at[0, s], b_send.at[k], b_recv.at[k], **to(d, peer)
        )

    def key_copy(k):
        peer = shifted(z, y, k)
        return pltpu.make_async_remote_copy(
            out.at[peer, pl.ds(2, 2)], pieces.at[pl.ds(1, 2), s], k_send.at[k], k_recv.at[k], **to(d, peer)
        )

    def give_context(k):
        context_of(k)
        context_copy(k).start()

    probs_of(0, 0, scores_of(0, 0))

    def two_forward(i, top):
        k = 2 * i
        later = scores_of(k + 2, 0)
        give_context(k)
        probs_of(k + 1, 1, top)
        last = scores_of(k + 3, 1)
        give_context(k + 1)
        probs_of(k + 2, 0, later)
        return last

    top = lax.fori_loop(0, blocks // 2 - 1, two_forward, scores_of(1, 1))
    give_context(blocks - 2)
    probs_of(blocks - 1, 1, top)
    context_of(blocks - 1)
    context[s] = out[s, 0]

    def arrive_grad(k, carry):
        head_copy(k).wait_recv()
        return carry

    lax.fori_loop(0, seq - 1, arrive_grad, 0)
    def give_query(k, slot):
        results_of(k, slot)
        query_copy(k).start()

    def two_backward(i, carry):
        k = 2 * i
        slopes_of(k + 1, 1)
        give_query(k, 0)
        slopes_of(k + 2, 0)
        give_query(k + 1, 1)
        return carry

    slopes_of(0, 0)
    lax.fori_loop(0, blocks // 4, two_backward, 0)

    def wait_context(k, carry):
        context_copy(k).wait_recv()
        return carry

    lax.fori_loop(0, seq - 1, wait_context, 0)

    def swap_copy(k):
        peer = (d + k) % runs
        return pltpu.make_async_remote_copy(
            context.at[pl.ds(peer * group, group)], swapped.at[d], s_send.at[k], s_recv.at[k], **to(peer, s)
        )

    def send_swap(k, carry):
        swap_copy(k).start()
        return carry

    lax.fori_loop(1, runs, send_swap, 0)
    swapped[d] = context[pl.ds(d * group, group)]
    lax.fori_loop(blocks // 4, blocks // 2 - 1, two_backward, 0)
    slopes_of(blocks - 1, 1)
    give_query(blocks - 2, 0)
    results_of(blocks - 1, 1)
    pieces[0, s] = out[s, 1]

    def wait_swap(k, carry):
        swap_copy(k).wait_recv()
        return carry

    lax.fori_loop(1, runs, wait_swap, 0)

    wide = 512

    def multiply(i, carry):
        at = pl.ds(pl.multiple_of(i * wide, wide), wide)
        left = jnp.concatenate([swapped[r].reshape(share, tokens) for r in range(runs)], 1)
        right = grads[:, :, at].reshape(runs * tokens, wide)
        total = jnp.dot(left, right, preferred_element_type=jnp.float32).astype(jnp.bfloat16)
        for k in range(heads):
            partial[k % 4, k // 4, :, at] = total[k * depth : (k + 1) * depth]
        return carry

    lax.fori_loop(0, model // wide, multiply, 0)

    def across_copy(k):
        peer = (y + k) % 4
        return pltpu.make_async_remote_copy(
            partial.at[peer], across.at[k], a_send.at[k], a_recv.at[k], **to(d, z * 4 + peer)
        )

    for k in range(1, 4):
        across_copy(k).start()

    def keys_of(u):
        total = parts[where[u, 0]]
        for r in range(1, blocks):
            total += parts[where[u, r]]
        out[u, 2:4] = total.T.astype(jnp.bfloat16).reshape(2, head, length)

    def give_keys(k, carry):
        keys_of(row(k))
        key_copy(k).start()
        return carry

    lax.fori_loop(0, seq - 1, give_keys, 0)
    keys_of(s)
    pieces[1:3, s] = out[s, 2:4]

    def attend(run, rows):
        left = context[pl.ds(run * group, group)].reshape(share, tokens).T
        return jnp.dot(left, rows, preferred_element_type=jnp.float32)

    def full_near(k, carry):
        run = chip(k) + core
        full_copy(run, 0, d).wait_recv()
        full_copy(run, 3 + k, other).start()
        attended[...] += attend(run, full_weight[run])
        return carry

    def full_other(k, carry):
        run = chip(k) + 1 - core
        full_copy(run, 0, d).wait_recv()
        attended[...] += attend(run, full_weight[run])
        return carry


    for k in range(1, 4):
        across_copy(k).wait_recv()

    def add_across(k, carry):
        total = partial[y, k].astype(jnp.float32)
        for i in range(1, 4):
            total += across[i, k].astype(jnp.float32)
        across[0, k] = total.astype(jnp.bfloat16)
        return carry

    def along_copy(k):
        peer = (z + k) % 8
        return pltpu.make_async_remote_copy(
            across.at[0, peer], along.at[k], l_send.at[k], l_recv.at[k], **to(d, peer * 4 + y)
        )

    def send_along(k, carry):
        along_copy(k).start()
        return carry

    lax.fori_loop(0, 8, add_across, 0)
    lax.fori_loop(1, 8, send_along, 0)
    attended[...] = attend(d, run_weight[...])
    lax.fori_loop(1, 4, full_near, 0)
    lax.fori_loop(0, 4, full_other, 0)

    def wait_along(k, carry):
        along_copy(k).wait_recv()
        return carry

    lax.fori_loop(1, 8, wait_along, 0)
    total = across[0, z].astype(jnp.float32)
    for k in range(1, 8):
        total += along[k].astype(jnp.float32)
    weight_grad[...] = total

    def finish_seq(k, carry):
        qkv_copy(k).wait_send()
        head_copy(k).wait_send()
        context_copy(k).wait_send()
        query_copy(k).wait()
        key_copy(k).wait()
        return carry

    lax.fori_loop(0, seq - 1, finish_seq, 0)

    def finish_swap(k, carry):
        swap_copy(k).wait_send()
        return carry

    def finish_along(k, carry):
        along_copy(k).wait_send()
        return carry

    lax.fori_loop(1, runs, finish_swap, 0)
    for k in range(1, 4):
        across_copy(k).wait_send()
    lax.fori_loop(1, 8, finish_along, 0)

    def finish_sent(k, carry):
        sent_copy((d + k) % runs, d).wait_send()
        return carry

    lax.fori_loop(1, runs, finish_sent, 0)

    def finish_weight(k, carry):
        weight_copy(s, k, s).wait_send()
        return carry

    lax.fori_loop(1, 32, finish_weight, 0)

    def finish_grads(k, carry):
        grad_copy(d, k, d).wait_send()
        return carry

    lax.fori_loop(0, 7, finish_grads, 0)

    def finish_full(k, carry):
        full_copy(d, k, other).wait_send()
        return carry

    lax.fori_loop(0, 7, finish_full, 0)


def layer(layout, where, weight, rows, upstream, mask, runs):
    tokens, model = upstream.shape
    picks, heads = layout.shape
    depth = weight.shape[0]
    group = heads // runs
    bf16, f32, dma = jnp.bfloat16, jnp.float32, pltpu.SemaphoreType.DMA
    vmem, smem = pl.BlockSpec(memory_space=pltpu.VMEM), pl.BlockSpec(memory_space=pltpu.SMEM)
    each, some = dma((heads,)), dma((8,))
    return pl.pallas_call(
        layer_kernel,
        name="layer",
        out_shape=(
            jax.ShapeDtypeStruct((tokens, model), f32),
            jax.ShapeDtypeStruct((3, heads, HS, tokens), bf16),
            jax.ShapeDtypeStruct((depth, model), f32),
        ),
        in_specs=[smem, smem] + [pl.BlockSpec(memory_space=pltpu.HBM)] * 4,
        out_specs=(vmem,) * 3,
        scratch_shapes=[
            pltpu.VMEM((heads, 3, HS, tokens), bf16),
            pltpu.VMEM((heads, HS, tokens), bf16),
            pltpu.VMEM((runs, tokens, model), bf16),
            pltpu.VMEM((heads * depth, model), bf16),
            pltpu.VMEM(rows.shape, bf16),
            pltpu.VMEM(upstream.shape, bf16),
            pltpu.VMEM(mask.shape, jnp.int32),
            pltpu.VMEM((heads, 3, HS, tokens), bf16),
            pltpu.VMEM((runs, group, HS, tokens), bf16),
            pltpu.VMEM((runs, group, HS, tokens), bf16),
            pltpu.VMEM((runs, heads * depth, model), bf16),
            pltpu.VMEM((heads, tokens, 2 * HS), bf16),
            pltpu.VMEM((heads * picks + 1, tokens, 2 * HS), f32),
            pltpu.VMEM((heads, picks * tokens, tokens), bf16),
            pltpu.VMEM((2, picks * tokens, tokens), bf16),
            pltpu.VMEM((2, picks, tokens, tokens), f32),
            pltpu.VMEM((heads, 4, HS, tokens), bf16),
            pltpu.VMEM((heads, HS, tokens), bf16),
            pltpu.VMEM((runs, group, HS, tokens), bf16),
            pltpu.VMEM((4, 8, depth, model), bf16),
            pltpu.VMEM((4, 8, depth, model), bf16),
            pltpu.VMEM((8, depth, model), bf16),
            dma((4,)), each, each, some, some, each, each, some, some, each, each,
            some, some, each, each, each, each, each, each,
            some, some, dma((4,)), dma((4,)), some, some,
        ],
        cost_estimate=pl.CostEstimate(
            flops=20 * heads * tokens * picks * tokens * HS, bytes_accessed=16 << 20, transcendentals=0
        ),
        compiler_params=pltpu.CompilerParams(
            collective_id=0, has_side_effects=True, vmem_limit_bytes=60 << 20
        ),
    )(layout, where, weight, rows, upstream, mask)


def on_device(projected, out_weight, upstream, peak_mask, block_layout):
    inner = projected.shape[2] // 3
    layout = block_layout[0].T
    picks, blocks = layout.shape
    index = jnp.arange(picks)[:, None] + picks * jnp.arange(blocks)
    same = layout[:, None] == jnp.arange(blocks)[None, :, None]
    where = jnp.min(jnp.where(same, index[:, None], blocks * picks), axis=0).astype(jnp.int32)
    attended, projected_grad, weight_grad = layer(
        layout, where, out_weight, projected[0], upstream[0], peak_mask, lax.axis_size("dp")
    )
    projected_grad = projected_grad.reshape(3 * inner, -1).T
    return (attended.astype(jnp.bfloat16)[None], projected_grad[None], weight_grad)


def solution(mesh):
    in_specs = (
        P("dp", "seq", None),
        P(("dp", "seq"), None),
        P("dp", "seq", None),
        P("dp", "seq"),
        P("seq", None, None),
    )
    out_specs = (P("dp", "seq", None), P("dp", "seq", None), P(("dp", "seq"), None))
    return jax.shard_map(
        on_device, mesh=mesh, in_specs=in_specs, out_specs=out_specs, check_vma=False
    )
```

```python
import jax
import jax.numpy as jnp
from jax import lax
from jax.experimental import pallas as pl
from jax.experimental.pallas import tpu as pltpu
from jax.sharding import PartitionSpec as P

HS = 64
SCALE = 0.125


MESH = pl.DeviceIdType.MESH


def place():
    d, s = lax.axis_index("dp"), lax.axis_index("seq")
    return d, d // 2, d % 2, s, s // 4, s % 4


def shifted(z, y, k):
    along, across = k // 4, k % 4
    along = 4 + (1 - along % 2 * 2) * ((along + 1) // 2)
    across = 2 + (1 - across % 2 * 2) * ((across + 1) // 2)
    return (z + along) % 8 * 4 + (y + across) % 4


def layer_kernel(
    layout, where, weight, rows_in, upstream_in, mask_in, attended, pieces, weight_grad,
    qkv, grad, grads, run_weight, rows, upstream, mask, turned, sent, mixed, full_weight,
    kvn, parts, probs, slopes, scores, out, context, swapped, partial, across, along,
    in_sem, w_send, w_recv, m_send, m_recv, q_send, q_recv, x_send, x_recv, g_send, g_recv,
    f_send, f_recv, c_send, c_recv, b_send, b_recv, k_send, k_recv,
    s_send, s_recv, a_send, a_recv, l_send, l_recv,
):
    d, x, core, s, z, y = place()
    tokens, model = upstream.shape
    heads, _, head, _ = qkv.shape
    seq, runs, depth = heads, grads.shape[0], weight.shape[0]
    group = heads // runs
    share = group * head
    other = d + 1 - 2 * core

    def to(dp, at):
        return {"device_id": (dp, at), "device_id_type": MESH}

    def weight_rows(at):
        return run_weight.at[pl.ds(pl.multiple_of(at * depth, depth), depth)]

    loads = [
        pltpu.make_async_copy(upstream_in, upstream, in_sem.at[0]),
        pltpu.make_async_copy(mask_in, mask, in_sem.at[1]),
        pltpu.make_async_copy(rows_in, rows, in_sem.at[2]),
        pltpu.make_async_copy(weight, weight_rows(s), in_sem.at[3]),
    ]
    for load in loads:
        load.start()
    barrier = pltpu.get_barrier_semaphore()

    def greet_seq(k, carry):
        pl.semaphore_signal(barrier, inc=1, **to(d, shifted(z, y, k)))
        return carry

    def greet_dp(k, carry):
        pl.semaphore_signal(barrier, inc=1, **to((d + k) % runs, s))
        return carry

    lax.fori_loop(0, seq - 1, greet_seq, 0)
    lax.fori_loop(1, runs, greet_dp, 0)
    loads[0].wait()
    loads[1].wait()
    column = jnp.broadcast_to(mask[...].astype(jnp.float32), (tokens, tokens)).T.astype(jnp.bfloat16)
    for i in range(model // tokens):
        part = slice(i * tokens, (i + 1) * tokens)
        grads[d, :, part] = upstream[:, part] * column

    def turn(pair, carry):
        for c in range(3):
            at = pl.multiple_of(c * (heads * head) + pair * 2 * head, 2 * head)
            both = rows[:, pl.ds(at, 2 * head)].T
            turned[2 * pair, c] = both[:head]
            turned[2 * pair + 1, c] = both[head:]
        return carry

    loads[2].wait()
    lax.fori_loop(0, heads // 2, turn, 0)
    loads[3].wait()

    pl.semaphore_wait(barrier, seq - 1 + runs - 1)

    def weight_copy(at, k, peer):
        return pltpu.make_async_remote_copy(
            weight_rows(at), weight_rows(at), w_send.at[k], w_recv.at[at], **to(d, peer)
        )

    def weight_z(k, carry):
        weight_copy(s, k, (z + k) % 8 * 4 + y).start()
        return carry

    lax.fori_loop(1, 8, weight_z, 0)

    def grad_copy(run, k, peer):
        return pltpu.make_async_remote_copy(
            grads.at[run], grads.at[run], m_send.at[k], m_recv.at[run], **to(peer, s)
        )

    def chip(k):
        return (x + k) % 4 * 2

    def grads_x(k, carry):
        grad_copy(d, k, chip(k) + core).start()
        return carry

    lax.fori_loop(1, 4, grads_x, 0)
    grad_copy(d, 0, d + 1 - 2 * core).start()

    def qkv_copy(k):
        peer = shifted(z, y, k)
        return pltpu.make_async_remote_copy(
            turned.at[peer], qkv.at[s], q_send.at[k], q_recv.at[k], **to(d, peer)
        )

    def send_qkv(k, carry):
        qkv_copy(k).start()
        return carry

    lax.fori_loop(0, seq - 1, send_qkv, 0)
    qkv[s] = turned[s]

    def weight_y(k, carry):
        at = (z + k) % 8 * 4 + y

        @pl.when(k > 0)
        def _():
            weight_copy(at, 0, s).wait_recv()

        for i in range(1, 4):
            weight_copy(at, 8 * i + k, z * 4 + (y + i) % 4).start()
        return carry

    lax.fori_loop(0, 8, weight_y, 0)

    def weight_wait(k, carry):
        for i in range(1, 4):
            weight_copy(k * 4 + (y + i) % 4, 0, s).wait_recv()
        return carry

    lax.fori_loop(0, 8, weight_wait, 0)

    def sent_copy(run, source):
        return pltpu.make_async_remote_copy(
            sent.at[run], mixed.at[source], x_send.at[run], x_recv.at[source], **to(run, s)
        )

    def one_run(run):
        value = lax.dot_general(
            run_weight[...], grads[run], (((1,), (1,)), ((), ())), preferred_element_type=jnp.float32
        )
        sent[run] = value.astype(jnp.bfloat16).reshape(heads // runs, head, tokens)

        @pl.when(run != d)
        def _():
            sent_copy(run, d).start()

    def runs_near(k, carry):
        run = chip(k) + core

        @pl.when(k > 0)
        def _():
            grad_copy(run, 0, d).wait_recv()
            grad_copy(run, 3 + k, d + 1 - 2 * core).start()

        one_run(run)
        return carry

    lax.fori_loop(0, 4, runs_near, 0)

    def runs_other(k, carry):
        run = chip(k) + 1 - core
        grad_copy(run, 0, d).wait_recv()
        one_run(run)
        return carry

    lax.fori_loop(0, 4, runs_other, 0)

    mixed[d] = sent[d]

    def full_copy(run, k, peer):
        source = run_weight if run is d else full_weight.at[run]
        return pltpu.make_async_remote_copy(
            source, full_weight.at[run], f_send.at[k], f_recv.at[run], **to(peer, s)
        )

    def full_x(k, carry):
        full_copy(d, k, chip(k) + core).start()
        return carry

    lax.fori_loop(1, 4, full_x, 0)
    full_copy(d, 0, other).start()

    def wait_mixed(k, carry):
        sent_copy(d, (d + k) % runs).wait_recv()
        return carry

    lax.fori_loop(1, runs, wait_mixed, 0)

    def head_copy(k):
        peer = shifted(z, y, k)
        return pltpu.make_async_remote_copy(
            mixed.at[peer // group, peer % group], grad.at[s], g_send.at[k], g_recv.at[k], **to(d, peer)
        )

    def send_head(k, carry):
        head_copy(k).start()
        return carry

    lax.fori_loop(0, seq - 1, send_head, 0)
    grad[s] = mixed[s // (heads // runs), s % (heads // runs)]

    def arrive_qkv(k, carry):
        qkv_copy(k).wait_recv()
        return carry

    lax.fori_loop(0, seq - 1, arrive_qkv, 0)

    blocks, length = heads, tokens
    picks = layout.shape[0]
    pair = 2 * head
    eighths = length // 8

    def prepare(b, carry):
        kvn[b] = qkv[b, 1:3].reshape(pair, length).T
        return carry

    lax.fori_loop(0, blocks, prepare, 0, unroll=4)
    parts[blocks * picks] = jnp.zeros((length, pair), jnp.float32)

    low = lax.broadcasted_iota(jnp.int32, (length, pair), 1) < head

    def picked(r):
        return [layout[j, r] for j in range(picks)]

    def row(k):
        return shifted(z, y, k)

    def scores_of(k, slot):
        q = qkv[row(k), 0] * jnp.bfloat16(SCALE)
        into = jnp.concatenate([q, jnp.zeros_like(q)], 0)
        top = None
        for j, b in enumerate(picked(row(k))):
            score = jnp.dot(kvn[b], into, preferred_element_type=jnp.float32)
            scores[slot, j] = score
            part = jnp.max(score.reshape(eighths, 8, length), axis=0)
            top = part if top is None else jnp.maximum(top, part)
        return jnp.max(top, axis=0, keepdims=True)

    def probs_of(k, slot, top):
        total = jnp.zeros((8, length), jnp.float32)
        for j in range(picks):
            e = jnp.exp(scores[slot, j] - top)
            scores[slot, j] = e
            total += jnp.sum(e.reshape(eighths, 8, length), axis=0)
        inverse = 1.0 / jnp.sum(total, axis=0, keepdims=True)
        for j in range(picks):
            probs[k, pl.ds(j * length, length)] = (scores[slot, j] * inverse).astype(jnp.bfloat16)

    def context_of(k):
        values = jnp.concatenate([qkv[b, 2] for b in picked(row(k))], 1)
        out[row(k), 0] = jnp.dot(
            values, probs[k], preferred_element_type=jnp.float32
        ).astype(jnp.bfloat16)

    def slopes_of(k, slot):
        g = grad[row(k)]
        into = jnp.concatenate([jnp.zeros_like(g), g], 0)
        delta = jnp.sum(
            g.astype(jnp.float32) * out[row(k), 0].astype(jnp.float32), axis=0, keepdims=True
        )
        for j, b in enumerate(picked(row(k))):
            rows = pl.ds(j * length, length)
            slope = jnp.dot(kvn[b], into, preferred_element_type=jnp.float32) - delta
            slope = probs[k, rows].astype(jnp.float32) * slope
            slopes[slot, rows] = slope.astype(jnp.bfloat16)

    def results_of(k, slot):
        r = row(k)
        keys = jnp.concatenate([qkv[b, 1] for b in picked(r)], 1)
        value = jnp.dot(keys, slopes[slot], preferred_element_type=jnp.float32)
        out[r, 1] = (value * SCALE).astype(jnp.bfloat16)
        turned = jnp.concatenate([qkv[r, 0] * jnp.bfloat16(SCALE), grad[r]], 0).T
        into = jnp.concatenate([jnp.where(low, turned, 0), jnp.where(low, 0, turned)], 0)
        for j in range(picks):
            rows = pl.ds(j * length, length)
            both = jnp.concatenate([slopes[slot, rows], probs[k, rows]], 1)
            parts[r * picks + j] = jnp.dot(both, into, preferred_element_type=jnp.float32)

    def context_copy(k):
        peer = shifted(z, y, k)
        return pltpu.make_async_remote_copy(
            out.at[peer, 0], context.at[s], c_send.at[k], c_recv.at[k], **to(d, peer)
        )

    def query_copy(k):
        peer = shifted(z, y, k)
        return pltpu.make_async_remote_copy(
            out.at[peer, 1], pieces.at[0, s], b_send.at[k], b_recv.at[k], **to(d, peer)
        )

    def key_copy(k):
        peer = shifted(z, y, k)
        return pltpu.make_async_remote_copy(
            out.at[peer, pl.ds(2, 2)], pieces.at[pl.ds(1, 2), s], k_send.at[k], k_recv.at[k], **to(d, peer)
        )

    def give_context(k):
        context_of(k)
        context_copy(k).start()

    probs_of(0, 0, scores_of(0, 0))

    def two_forward(i, top):
        k = 2 * i
        later = scores_of(k + 2, 0)
        give_context(k)
        probs_of(k + 1, 1, top)
        last = scores_of(k + 3, 1)
        give_context(k + 1)
        probs_of(k + 2, 0, later)
        return last

    top = lax.fori_loop(0, blocks // 2 - 1, two_forward, scores_of(1, 1))
    give_context(blocks - 2)
    probs_of(blocks - 1, 1, top)
    context_of(blocks - 1)
    context[s] = out[s, 0]

    def arrive_grad(k, carry):
        head_copy(k).wait_recv()
        return carry

    lax.fori_loop(0, seq - 1, arrive_grad, 0)
    def give_query(k, slot):
        results_of(k, slot)
        query_copy(k).start()

    def two_backward(i, carry):
        k = 2 * i
        slopes_of(k + 1, 1)
        give_query(k, 0)
        slopes_of(k + 2, 0)
        give_query(k + 1, 1)
        return carry

    slopes_of(0, 0)
    lax.fori_loop(0, blocks // 4, two_backward, 0)

    def wait_context(k, carry):
        context_copy(k).wait_recv()
        return carry

    lax.fori_loop(0, seq - 1, wait_context, 0)

    def swap_copy(k):
        peer = (d + k) % runs
        return pltpu.make_async_remote_copy(
            context.at[pl.ds(peer * group, group)], swapped.at[d], s_send.at[k], s_recv.at[k], **to(peer, s)
        )

    def send_swap(k, carry):
        swap_copy(k).start()
        return carry

    lax.fori_loop(1, runs, send_swap, 0)
    swapped[d] = context[pl.ds(d * group, group)]
    lax.fori_loop(blocks // 4, blocks // 2 - 1, two_backward, 0)
    slopes_of(blocks - 1, 1)
    give_query(blocks - 2, 0)
    results_of(blocks - 1, 1)
    pieces[0, s] = out[s, 1]

    def wait_swap(k, carry):
        swap_copy(k).wait_recv()
        return carry

    lax.fori_loop(1, runs, wait_swap, 0)

    wide = 512

    def multiply(i, carry):
        at = pl.ds(pl.multiple_of(i * wide, wide), wide)
        left = jnp.concatenate([swapped[r].reshape(share, tokens) for r in range(runs)], 1)
        right = grads[:, :, at].reshape(runs * tokens, wide)
        total = jnp.dot(left, right, preferred_element_type=jnp.float32).astype(jnp.bfloat16)
        for k in range(heads):
            partial[k % 4, k // 4, :, at] = total[k * depth : (k + 1) * depth]
        return carry

    lax.fori_loop(0, model // wide, multiply, 0)

    def across_copy(k):
        peer = (y + k) % 4
        return pltpu.make_async_remote_copy(
            partial.at[peer], across.at[k], a_send.at[k], a_recv.at[k], **to(d, z * 4 + peer)
        )

    for k in range(1, 4):
        across_copy(k).start()

    def keys_of(u):
        total = parts[where[u, 0]]
        for r in range(1, blocks):
            total += parts[where[u, r]]
        out[u, 2:4] = total.T.astype(jnp.bfloat16).reshape(2, head, length)

    def give_keys(k, carry):
        keys_of(row(k))
        key_copy(k).start()
        return carry

    lax.fori_loop(0, seq - 1, give_keys, 0)
    keys_of(s)
    pieces[1:3, s] = out[s, 2:4]

    def attend(run, rows):
        left = context[pl.ds(run * group, group)].reshape(share, tokens).T
        return jnp.dot(left, rows, preferred_element_type=jnp.float32)

    def full_near(k, carry):
        run = chip(k) + core
        full_copy(run, 0, d).wait_recv()
        full_copy(run, 3 + k, other).start()
        attended[...] += attend(run, full_weight[run])
        return carry

    def full_other(k, carry):
        run = chip(k) + 1 - core
        full_copy(run, 0, d).wait_recv()
        attended[...] += attend(run, full_weight[run])
        return carry


    attended[...] = attend(d, run_weight[...])
    lax.fori_loop(1, 4, full_near, 0)
    for k in range(1, 4):
        across_copy(k).wait_recv()

    def add_across(k, carry):
        total = partial[y, k].astype(jnp.float32)
        for i in range(1, 4):
            total += across[i, k].astype(jnp.float32)
        across[0, k] = total.astype(jnp.bfloat16)
        return carry

    def along_copy(k):
        peer = (z + k) % 8
        return pltpu.make_async_remote_copy(
            across.at[0, peer], along.at[k], l_send.at[k], l_recv.at[k], **to(d, peer * 4 + y)
        )

    def send_along(k, carry):
        along_copy(k).start()
        return carry

    lax.fori_loop(0, 8, add_across, 0)
    lax.fori_loop(1, 8, send_along, 0)
    lax.fori_loop(0, 4, full_other, 0)

    def wait_along(k, carry):
        along_copy(k).wait_recv()
        return carry

    lax.fori_loop(1, 8, wait_along, 0)
    total = across[0, z].astype(jnp.float32)
    for k in range(1, 8):
        total += along[k].astype(jnp.float32)
    weight_grad[...] = total

    def finish_seq(k, carry):
        qkv_copy(k).wait_send()
        head_copy(k).wait_send()
        context_copy(k).wait_send()
        query_copy(k).wait()
        key_copy(k).wait()
        return carry

    lax.fori_loop(0, seq - 1, finish_seq, 0)

    def finish_swap(k, carry):
        swap_copy(k).wait_send()
        return carry

    def finish_along(k, carry):
        along_copy(k).wait_send()
        return carry

    lax.fori_loop(1, runs, finish_swap, 0)
    for k in range(1, 4):
        across_copy(k).wait_send()
    lax.fori_loop(1, 8, finish_along, 0)

    def finish_sent(k, carry):
        sent_copy((d + k) % runs, d).wait_send()
        return carry

    lax.fori_loop(1, runs, finish_sent, 0)

    def finish_weight(k, carry):
        weight_copy(s, k, s).wait_send()
        return carry

    lax.fori_loop(1, 32, finish_weight, 0)

    def finish_grads(k, carry):
        grad_copy(d, k, d).wait_send()
        return carry

    lax.fori_loop(0, 7, finish_grads, 0)

    def finish_full(k, carry):
        full_copy(d, k, other).wait_send()
        return carry

    lax.fori_loop(0, 7, finish_full, 0)


def layer(layout, where, weight, rows, upstream, mask, runs):
    tokens, model = upstream.shape
    picks, heads = layout.shape
    depth = weight.shape[0]
    group = heads // runs
    bf16, f32, dma = jnp.bfloat16, jnp.float32, pltpu.SemaphoreType.DMA
    vmem, smem = pl.BlockSpec(memory_space=pltpu.VMEM), pl.BlockSpec(memory_space=pltpu.SMEM)
    each, some = dma((heads,)), dma((8,))
    return pl.pallas_call(
        layer_kernel,
        name="layer",
        out_shape=(
            jax.ShapeDtypeStruct((tokens, model), f32),
            jax.ShapeDtypeStruct((3, heads, HS, tokens), bf16),
            jax.ShapeDtypeStruct((depth, model), f32),
        ),
        in_specs=[smem, smem] + [pl.BlockSpec(memory_space=pltpu.HBM)] * 4,
        out_specs=(vmem,) * 3,
        scratch_shapes=[
            pltpu.VMEM((heads, 3, HS, tokens), bf16),
            pltpu.VMEM((heads, HS, tokens), bf16),
            pltpu.VMEM((runs, tokens, model), bf16),
            pltpu.VMEM((heads * depth, model), bf16),
            pltpu.VMEM(rows.shape, bf16),
            pltpu.VMEM(upstream.shape, bf16),
            pltpu.VMEM(mask.shape, jnp.int32),
            pltpu.VMEM((heads, 3, HS, tokens), bf16),
            pltpu.VMEM((runs, group, HS, tokens), bf16),
            pltpu.VMEM((runs, group, HS, tokens), bf16),
            pltpu.VMEM((runs, heads * depth, model), bf16),
            pltpu.VMEM((heads, tokens, 2 * HS), bf16),
            pltpu.VMEM((heads * picks + 1, tokens, 2 * HS), f32),
            pltpu.VMEM((heads, picks * tokens, tokens), bf16),
            pltpu.VMEM((2, picks * tokens, tokens), bf16),
            pltpu.VMEM((2, picks, tokens, tokens), f32),
            pltpu.VMEM((heads, 4, HS, tokens), bf16),
            pltpu.VMEM((heads, HS, tokens), bf16),
            pltpu.VMEM((runs, group, HS, tokens), bf16),
            pltpu.VMEM((4, 8, depth, model), bf16),
            pltpu.VMEM((4, 8, depth, model), bf16),
            pltpu.VMEM((8, depth, model), bf16),
            dma((4,)), each, each, some, some, each, each, some, some, each, each,
            some, some, each, each, each, each, each, each,
            some, some, dma((4,)), dma((4,)), some, some,
        ],
        cost_estimate=pl.CostEstimate(
            flops=20 * heads * tokens * picks * tokens * HS, bytes_accessed=16 << 20, transcendentals=0
        ),
        compiler_params=pltpu.CompilerParams(
            collective_id=0, has_side_effects=True, vmem_limit_bytes=60 << 20
        ),
    )(layout, where, weight, rows, upstream, mask)


def on_device(projected, out_weight, upstream, peak_mask, block_layout):
    inner = projected.shape[2] // 3
    layout = block_layout[0].T
    picks, blocks = layout.shape
    index = jnp.arange(picks)[:, None] + picks * jnp.arange(blocks)
    same = layout[:, None] == jnp.arange(blocks)[None, :, None]
    where = jnp.min(jnp.where(same, index[:, None], blocks * picks), axis=0).astype(jnp.int32)
    attended, projected_grad, weight_grad = layer(
        layout, where, out_weight, projected[0], upstream[0], peak_mask, lax.axis_size("dp")
    )
    projected_grad = projected_grad.reshape(3 * inner, -1).T
    return (attended.astype(jnp.bfloat16)[None], projected_grad[None], weight_grad)


def solution(mesh):
    in_specs = (
        P("dp", "seq", None),
        P(("dp", "seq"), None),
        P("dp", "seq", None),
        P("dp", "seq"),
        P("seq", None, None),
    )
    out_specs = (P("dp", "seq", None), P("dp", "seq", None), P(("dp", "seq"), None))
    return jax.shard_map(
        on_device, mesh=mesh, in_specs=in_specs, out_specs=out_specs, check_vma=False
    )
```
